32 devices in a mesh: groups: 2 (over x), feat: 16 (over z, y, core).
Axes of the slice: x: 2, y: 2, z: 4, core: 2. Of those that a mesh axis runs over, the one named last changes fastest.
Arguments:
- design: float32 [1024, 32768], P('groups', 'feat'), parts along dimension 0, may hold values from -6 to 6
- targets: float32 [1024, 128], P('groups'), parts along dimension 0, may hold values from -6 to 6
- coef_now: float32 [65536, 128], P(('groups', 'feat')), parts along dimension 0, may hold values from -1 to 1
- coef_prev: float32 [65536, 128], P(('groups', 'feat')), parts along dimension 0, may hold values from -1 to 1
- penalty: float32 [256], P('groups'), parts along dimension 0, may hold values from 0.1 to 1
- drop_mask: int32 [512], P(('groups', 'feat')), parts along dimension 0, may hold values from 0 to 1, as said below
- dest_shard: int32 [512], P(('groups', 'feat')), parts along dimension 0, may hold values from 0 to 15, as said below
Outputs:
- coef_out: float32 [98304, 128], P(('groups', 'feat')), parts along dimension 0
- design_out: float32 [1024, 49152], P('groups', 'feat'), parts along dimension 0
- duality_gap: float32 [256], P('groups'), parts along dimension 0
- dual_value: float32 [256], P('groups'), parts along dimension 0
- coef_l1: float32 [256], P('groups'), parts along dimension 0
The draws below stay inside these ranges and needn't reach their ends.
There are 2 independent parts, one for each index of `groups`. The reference program is written for one: setup_inputs(seed, part) draws one part's arguments, and reference() takes and returns one part's arrays. A program takes and returns all parts, laid end to end along the dimension named above; each array names one. Nothing has to cross between parts.
Inputs may be any that keep to these rules, and one draw needn't show every extreme that they name: `drop_mask`: screening marks blocks to drop with 1; shards drop very different shares of their blocks. `dest_shard`: a block's destination is its own shard, except that any of the first 4 blocks of a shard may go to the shard before it (cyclically) and any of the last 4 blocks to the shard after it; no shard receives more than 24 surviving blocks, and some shard receives exactly 24 in every draw.
All inputs are finite; a program needn't handle non-finite values.
Results may differ from the reference program's by a relative error of at most 0.0003.
Values sent between devices are 32-bit elements; how exact they have to be, the bound alone decides.
No kernel may reach another device: no remote copies, remote signals or barrier semaphores. Data moves between devices by JAX's collectives and lax.ppermute only.
A program may use at most 64 MiB of HBM per device.

```python
import math
import jax
import jax.numpy as jnp
from jax import lax

NSAMP = 512
PHENO = 128
START = 40
BLK_DEV = 16
EDGE = 4
SLOTS = 24
FEATURES = 32768
NBLOCKS = 256


def block_layout(key):
    shards = NBLOCKS // BLK_DEV
    base = jax.random.fold_in(key, 9137)
    key_star, key_level, key_rolled, key_sideways = jax.random.split(base, 4)
    star = jax.random.randint(key_star, (), 0, shards)
    levels = jax.random.randint(key_level, (shards, 1), 0, 4)
    rolled = jax.random.randint(key_rolled, (shards, BLK_DEV), 0, 8)
    sideways = jax.random.randint(key_sideways, (shards, BLK_DEV), 0, 2)
    position = jnp.arange(BLK_DEV)[None, :]
    owners = jnp.arange(shards)[:, None]
    dropped = rolled < 2 * levels
    offsets = jnp.where(position < EDGE, -sideways, jnp.where(position >= BLK_DEV - EDGE, sideways, 0))
    at_star = owners == star
    before_star = (owners == (star + shards - 1) % shards) & (position >= BLK_DEV - EDGE)
    after_star = (owners == (star + 1) % shards) & (position < EDGE)
    forced = at_star | before_star | after_star
    dropped = jnp.where(forced, False, dropped)
    offsets = jnp.where(at_star, 0, jnp.where(before_star, 1, jnp.where(after_star, -1, offsets)))
    targets_of = (owners + offsets + shards) % shards
    return (dropped.astype(jnp.int32).reshape(-1), targets_of.astype(jnp.int32).reshape(-1))


def draw_drop_mask(key, part):
    return block_layout(key)[0]


def draw_dest_shard(key, part):
    return block_layout(key)[1]


def sparse_coefficients(key, which):
    support_key = jax.random.fold_in(key, 4411)
    keep = jax.random.bernoulli(support_key, 0.01, (FEATURES, PHENO))
    value_key = jax.random.fold_in(key, which)
    position = jnp.arange(FEATURES, dtype=jnp.float32)[:, None] / FEATURES
    rise = 1.0 + 3.0 * position
    values = jnp.clip(jax.random.normal(value_key, (FEATURES, PHENO), jnp.float32), -4.0, 4.0)
    return jnp.where(keep, 0.02 * rise * values, 0.0).astype(jnp.float32)


def draw_coef_now(key, part):
    return sparse_coefficients(key, 731)


def draw_coef_prev(key, part):
    return sparse_coefficients(key, 857)


def block_levels(rng, shape, pieces, least, largest):
    loudness = 1.0
    for dim, parts in pieces:
        heights = jax.random.uniform(jax.random.fold_in(jax.random.fold_in(rng, 6), dim), (parts,), jnp.float32, least / len(pieces), largest / len(pieces))
        loudness = loudness * jnp.repeat(jnp.exp(heights), shape[dim] // parts).reshape((-1,) + (1,) * (len(shape) - 1 - dim))
    return loudness


def scatter_about(rng, extent, width, reach, cuts=(), kind=jnp.bfloat16):
    entries = jax.random.normal(rng, extent, jnp.float32) * width
    if len(cuts) > 0:
        entries = block_levels(rng, extent, cuts, -0.22, 0.18) * entries
    return jnp.clip(entries, min=-reach, max=reach).astype(kind)


def setup_inputs(seed: int = 0, part: int = 0) -> dict:
    keys = jax.random.split(jax.random.key(seed), 8)
    part_splits = jax.random.split(jax.random.fold_in(keys[7], part), 8)
    design = scatter_about(part_splits[0], (NSAMP, FEATURES), 1.0, 6.0, ((1, 16),), jnp.float32)
    targets = scatter_about(part_splits[1], (NSAMP, PHENO), 1.0, 6.0, (), jnp.float32)
    coef_now = draw_coef_now(jax.random.fold_in(jax.random.fold_in(keys[7], part), 71), part)
    coef_prev = draw_coef_prev(jax.random.fold_in(jax.random.fold_in(keys[7], part), 71), part)
    penalty = jnp.clip(jnp.exp(jax.random.uniform(part_splits[4], (PHENO,), jnp.float32, math.log(0.1), math.log(1.0))), 0.1, 1.0)
    drop_mask = draw_drop_mask(jax.random.fold_in(jax.random.fold_in(keys[7], part), 71), part)
    dest_shard = draw_dest_shard(jax.random.fold_in(jax.random.fold_in(keys[7], part), 71), part)
    return {"design": design, "targets": targets, "coef_now": coef_now, "coef_prev": coef_prev, "penalty": penalty, "drop_mask": drop_mask, "dest_shard": dest_shard}


precise = lax.Precision.HIGHEST

def shrink(values, level):
    return jnp.sign(values) * jnp.maximum(jnp.abs(values) - level, 0.0)

def reference(design, targets, coef_now, coef_prev, penalty, drop_mask, dest_shard):
    lipschitz = (math.sqrt(NSAMP) + math.sqrt(FEATURES)) ** 2
    level = penalty * (NSAMP / lipschitz)
    first_push = (START - 1) / (START + 2)
    second_push = START / (START + 3)

    def fitted(point):
        return jnp.dot(design, point, precision=precise, preferred_element_type=jnp.float32)

    def correlate(misfit):
        return lax.dot_general(design, misfit, (((0,), (0,)), ((), ())), precision=precise, preferred_element_type=jnp.float32)

    def descend(point):
        misfit = fitted(point) - targets
        return shrink(point - correlate(misfit) / lipschitz, level)
    coef_one = descend(coef_now + first_push * (coef_now - coef_prev))
    coef_two = descend(coef_one + second_push * (coef_one - coef_now))
    residual = targets - fitted(coef_two)
    correlation = correlate(residual)
    peak = lax.optimization_barrier(jnp.max(jnp.abs(correlation), axis=0))
    coef_l1 = lax.optimization_barrier(jnp.sum(jnp.abs(coef_two), axis=0))
    dual_scale = jnp.maximum(penalty, peak / NSAMP)
    dual_point = targets - penalty * residual / dual_scale
    dual_value = (lax.optimization_barrier(jnp.sum(targets * targets, axis=0)) - lax.optimization_barrier(jnp.sum(dual_point * dual_point, axis=0))) / (2.0 * NSAMP)
    primal = lax.optimization_barrier(jnp.sum(residual * residual, axis=0)) / (2.0 * NSAMP) + penalty * coef_l1
    duality_gap = primal - dual_value
    shards = NBLOCKS // BLK_DEV
    design_blocks = design.reshape(NSAMP, shards, BLK_DEV, 128)
    coef_blocks = coef_two.reshape(shards, BLK_DEV, 128, PHENO)
    survive = (drop_mask == 0).reshape(shards, BLK_DEV)
    destination = dest_shard.reshape(shards, BLK_DEV)
    owners = jnp.arange(shards, dtype=jnp.int32)[:, None]
    staying = survive & (destination == owners)
    to_right = survive & (destination == (owners + 1) % shards)
    to_left = survive & (destination == (owners + shards - 1) % shards)
    arrived = jnp.concatenate([jnp.roll(to_right, 1, axis=0)[:, BLK_DEV - EDGE:], staying, jnp.roll(to_left, -1, axis=0)[:, :EDGE]], axis=1).astype(jnp.int32)
    slot_of = jnp.cumsum(arrived, axis=1, dtype=jnp.int32) - 1
    placement = ((slot_of[:, :, None] == jnp.arange(SLOTS, dtype=jnp.int32)[None, None, :]) & (arrived[:, :, None] > 0)).astype(jnp.float32)
    design_cands = jnp.concatenate([jnp.roll(design_blocks, 1, axis=1)[:, :, BLK_DEV - EDGE:], design_blocks, jnp.roll(design_blocks, -1, axis=1)[:, :, :EDGE]], axis=2)
    design_out = jnp.einsum('nscf,scj->nsjf', design_cands, placement, precision=precise).reshape(NSAMP, shards * SLOTS * 128)
    coef_cands = jnp.concatenate([jnp.roll(coef_blocks, 1, axis=0)[:, BLK_DEV - EDGE:], coef_blocks, jnp.roll(coef_blocks, -1, axis=0)[:, :EDGE]], axis=1)
    coef_out = jnp.einsum('scfk,scj->sjfk', coef_cands, placement, precision=precise).reshape(shards * SLOTS * 128, PHENO)
    return (coef_out, design_out, duality_gap, dual_value, coef_l1)
```

```python
import functools
import math

import jax
import jax.numpy as jnp
from jax import lax
from jax.experimental import pallas as pl
from jax.experimental.pallas import tpu as pltpu
from jax.sharding import PartitionSpec as P

START = 40
LANE = 128
AXIS = "feat"


def swap(value, bit):
    count = lax.axis_size(AXIS)
    return lax.ppermute(value, AXIS, [(i, i ^ bit) for i in range(count)])


def stages(count):
    return [1 << s for s in range(count.bit_length() - 1)]


def halves(values):
    high = values.astype(jnp.bfloat16)
    low = (values - high.astype(jnp.float32)).astype(jnp.bfloat16)
    return high, low


def mul(left, right):
    return lax.dot_general(left, right, (((1,), (0,)), ((), ())), preferred_element_type=jnp.float32)


def shrink(values, level):
    return values - jnp.clip(values, -level, level)


def forward(high, low, point):
    width = point.shape[1]
    ph, plo = halves(point)
    both = mul(high, jnp.concatenate([ph, plo], axis=1))
    return both[:, :width] + both[:, width:] + mul(low, ph)


def backward(high, low, turned):
    width = turned.shape[0] // 2
    both = mul(turned, high)
    return both[:width] + both[width:] + mul(turned[:width], low)


def hand_over(parity, total, keep_ref, send_ref):
    half = keep_ref.shape[0]
    keep_ref[...] = total[pl.ds(pl.multiple_of(parity * half, 8), half), :]
    send_ref[...] = total[pl.ds(pl.multiple_of((1 - parity) * half, 8), half), :]


def take_over(parity, own_ref, other_ref, targets_ref, turned, whole):
    half = own_ref.shape[0]
    whole[pl.ds(pl.multiple_of(parity * half, 8), half), :] = own_ref[...]
    whole[pl.ds(pl.multiple_of((1 - parity) * half, 8), half), :] = other_ref[...]
    width = targets_ref.shape[1]
    misfit = whole[...] - targets_ref[...]
    across = misfit.T
    high, low = halves(across)
    turned[:width] = high
    turned[width:] = low
    return misfit


def first_kernel(push, flags_ref, parity_ref, design_ref, now_ref, prev_ref, keep_ref, send_ref, near_ref, far_ref, total):
    step = pl.program_id(0)
    last = pl.num_programs(0) - 1
    parity = parity_ref[0]
    block = design_ref[...]
    high, low = halves(block)
    now = now_ref[...]
    part = forward(high, low, now + push * (now - prev_ref[...]))
    rows = block.shape[0]
    edge = block.shape[1] // LANE

    @pl.when(step == 0)
    def _():
        total[...] = part

    @pl.when(step > 0)
    def _():
        total[...] += part

    def put(ref, side):
        ref[:rows, :] = block
        for k in range(edge):
            flag = flags_ref[side * edge + k]
            ref[rows:, k * LANE : (k + 1) * LANE] = jnp.full((8, LANE), flag, jnp.float32)

    @pl.when((step == 0) & (parity == 1))
    def _():
        put(near_ref, 0)

    @pl.when((step == 0) & (parity == 0))
    def _():
        put(far_ref, 0)

    @pl.when((step == last) & (parity == 0))
    def _():
        put(near_ref, 1)

    @pl.when((step == last) & (parity == 1))
    def _():
        put(far_ref, 1)

    @pl.when(step == last)
    def _():
        hand_over(parity, total, keep_ref, send_ref)


def descend_kernel(
    push_in, push_out, scale, level_scale, parity_ref, design_ref, later_ref, early_ref, own_ref, other_ref, targets_ref,
    penalty_ref, coef_ref, keep_ref, send_ref, mass_ref, total, turned,
):
    step = pl.program_id(0)
    parity = parity_ref[0]

    @pl.when(step == 0)
    def _():
        take_over(parity, own_ref, other_ref, targets_ref, turned, total)

    high, low = halves(design_ref[...])
    turn = backward(high, low, turned[...])
    later = later_ref[...]
    point = later + push_in * (later - early_ref[...])
    coef = shrink(point - turn.T * (1.0 / scale), penalty_ref[...] * level_scale)
    coef_ref[...] = coef
    mass = jnp.sum(jnp.abs(coef), axis=0, keepdims=True)
    if push_out is not None:
        part = forward(high, low, coef + push_out * (coef - later))
    else:
        part = forward(high, low, coef)

    @pl.when(step == 0)
    def _():
        total[...] = part
        mass_ref[...] = jnp.broadcast_to(mass, mass_ref.shape)

    @pl.when(step > 0)
    def _():
        total[...] += part
        mass_ref[...] += jnp.broadcast_to(mass, mass_ref.shape)

    @pl.when(step == pl.num_programs(0) - 1)
    def _():
        hand_over(parity, total, keep_ref, send_ref)


def peak_kernel(parity_ref, design_ref, own_ref, other_ref, targets_ref, peak_ref, square_ref, cross_ref, total, turned, best):
    step = pl.program_id(0)
    parity = parity_ref[0]

    @pl.when(step == 0)
    def _():
        residual = -take_over(parity, own_ref, other_ref, targets_ref, turned, total)
        square_ref[...] = jnp.sum(residual * residual, axis=0, keepdims=True)
        cross_ref[...] = jnp.sum(residual * targets_ref[...], axis=0, keepdims=True)
        best[...] = jnp.zeros_like(best)

    high, low = halves(design_ref[...])
    turn = jnp.abs(backward(high, low, turned[...]))
    for k in range(turn.shape[1] // LANE):
        best[...] = jnp.maximum(best[...], turn[:, k * LANE : (k + 1) * LANE])

    @pl.when(step == pl.num_programs(0) - 1)
    def _():
        peak_ref[...] = jnp.broadcast_to(jnp.max(best[...].T, axis=0, keepdims=True), peak_ref.shape)


def place_kernel(edge, along, table_ref, parity_ref, near_ref, own_ref, far_ref, out_ref, blank, sems):
    slots = table_ref.shape[0]
    own = slots - 2 * edge
    parity = parity_ref[0]
    blank[...] = jnp.zeros_like(blank)

    def piece(ref, index):
        start = pl.multiple_of(index * LANE, LANE)
        if along == 1:
            return ref.at[0 : out_ref.shape[0], pl.ds(start, LANE)]
        return ref.at[pl.ds(start, LANE), :]

    def copy(slot, src):
        return pltpu.make_async_copy(src, piece(out_ref, slot), sems.at[slot])

    for slot in range(slots):
        source = table_ref[slot]
        left = (source >= 0) & (source < edge)
        right = source >= edge + own
        from_near = (left & (parity == 1)) | (right & (parity == 0))
        from_far = (left & (parity == 0)) | (right & (parity == 1))
        inner = jnp.where(left, source, source - edge - own)

        @pl.when(source < 0)
        def _():
            copy(slot, blank).start()

        @pl.when((source >= edge) & (source < edge + own))
        def _():
            copy(slot, piece(own_ref, source - edge)).start()

        @pl.when(from_near)
        def _():
            copy(slot, piece(near_ref, inner)).start()

        @pl.when(from_far)
        def _():
            copy(slot, piece(far_ref, inner)).start()

    for slot in range(slots):
        copy(slot, blank).wait()


VM = pltpu.MemorySpace.VMEM
SM = pltpu.MemorySpace.SMEM


def whole():
    return pl.BlockSpec(memory_space=VM)


def scalars():
    return pl.BlockSpec(memory_space=SM)


def f32(*shape):
    return jax.ShapeDtypeStruct(shape, jnp.float32)


def fixed(shape):
    return pl.BlockSpec(shape, lambda i: (0,) * len(shape))


def local(design, targets, coef_now, coef_prev, penalty, drop_mask, dest_shard):
    samples, feats = design.shape
    width = targets.shape[1]
    shards = lax.axis_size(AXIS)
    me = lax.axis_index(AXIS)
    parity = (me & 1).astype(jnp.int32).reshape(1)
    lipschitz = (math.sqrt(samples) + math.sqrt(feats * shards)) ** 2
    first_push = (START - 1) / (START + 2)
    second_push = START / (START + 3)
    blocks = feats // LANE
    edge = blocks // 4
    chunk = edge * LANE
    steps = feats // chunk
    half = samples // 2

    survive = drop_mask == 0
    to_left = survive[:edge] & (dest_shard[:edge] == (me + shards - 1) % shards)
    to_right = survive[blocks - edge :] & (dest_shard[blocks - edge :] == (me + 1) % shards)
    staying = survive & (dest_shard == me)
    flags = jnp.concatenate([to_left, to_right]).astype(jnp.float32)

    def feat_spec():
        return pl.BlockSpec((samples, chunk), lambda i: (0, i))

    def coef_spec():
        return pl.BlockSpec((chunk, width), lambda i: (i, 0))

    params = pltpu.CompilerParams(vmem_limit_bytes=24 << 20, dimension_semantics=("arbitrary",))
    row_spec = fixed((1, width))
    half_spec = fixed((half, width))

    keep, send, near, far = pl.pallas_call(
        functools.partial(first_kernel, first_push),
        grid=(steps,),
        in_specs=[scalars(), scalars(), feat_spec(), coef_spec(), coef_spec()],
        out_specs=[half_spec, half_spec, fixed((samples + 8, chunk)), fixed((samples + 8, chunk))],
        out_shape=[f32(half, width)] * 2 + [f32(samples + 8, chunk)] * 2,
        scratch_shapes=[pltpu.VMEM((samples, width), jnp.float32)],
        compiler_params=params,
        name="first",
    )(flags, parity, design, coef_now, coef_prev)

    def outward(value):
        count = lax.axis_size(AXIS)
        pairs = [(i, (i + 1) % count if i % 2 else (i - 1) % count) for i in range(count)]
        return lax.ppermute(value, AXIS, pairs)

    def combine(keep, send, rows):
        total = keep + swap(send, 1)
        for bit in stages(shards)[1:]:
            total = total + swap(total, bit)
        other = swap(total[:rows], 1)
        return total, other

    near_in = swap(near, 1)
    far_in = outward(far)

    turned = pltpu.VMEM((2 * width, samples), jnp.bfloat16)
    sum_scratch = pltpu.VMEM((samples, width), jnp.float32)

    def descend(push_in, push_out, later, early, own, other):
        return pl.pallas_call(
            functools.partial(descend_kernel, push_in, push_out, lipschitz, samples / lipschitz),
            grid=(steps,),
            in_specs=[scalars(), feat_spec(), coef_spec(), coef_spec(), half_spec, half_spec, fixed((samples, width)), row_spec],
            out_specs=[coef_spec(), half_spec, half_spec, fixed((8, width))],
            out_shape=[f32(feats, width), f32(half, width), f32(half, width), f32(8, width)],
            scratch_shapes=[sum_scratch, turned],
            compiler_params=params,
            name="descend",
        )(parity, design, later, early, own, other, targets, penalty.reshape(1, width))

    own, other = combine(keep, send, half)
    coef_one, keep, send, _ = descend(first_push, second_push, coef_now, coef_prev, own, other)
    own, other = combine(keep, send, half)
    coef_two, keep, send, mass = descend(second_push, None, coef_one, coef_now, own, other)

    odd = (me & 1) == 1
    left_edge, right_edge = coef_two[:chunk], coef_two[feats - chunk :]
    near_coef = swap(jnp.where(odd, left_edge, right_edge), 1)
    far_coef = outward(jnp.where(odd, right_edge, left_edge))

    own, other = combine(jnp.concatenate([keep, mass]), jnp.concatenate([send, mass]), half)
    mass = own[half]
    own = own[:half]
    peak, square, cross = pl.pallas_call(
        peak_kernel,
        grid=(steps,),
        in_specs=[scalars(), feat_spec(), half_spec, half_spec, fixed((samples, width))],
        out_specs=[fixed((8, width)), row_spec, row_spec],
        out_shape=[f32(8, width), f32(1, width), f32(1, width)],
        scratch_shapes=[sum_scratch, turned, pltpu.VMEM((width, LANE), jnp.float32)],
        compiler_params=params,
        name="peak",
    )(parity, design, own, other, targets)
    for bit in stages(shards):
        peak = jnp.maximum(peak, swap(peak, bit))

    dual_scale = jnp.maximum(penalty, peak[0] / samples)
    ratio = penalty / dual_scale
    dual_value = (2.0 * ratio * cross[0] - ratio * ratio * square[0]) / (2.0 * samples)
    duality_gap = square[0] / (2.0 * samples) + penalty * mass - dual_value

    near_flags = near_in[samples, ::LANE] > 0.5
    far_flags = far_in[samples, ::LANE] > 0.5
    before = jnp.where(odd, near_flags, far_flags)
    after = jnp.where(odd, far_flags, near_flags)
    arrived = jnp.concatenate([before, staying, after]).astype(jnp.int32)
    slots = blocks + 2 * edge
    slot_of = jnp.cumsum(arrived, dtype=jnp.int32) - 1
    ids = jnp.arange(slots, dtype=jnp.int32)
    hit = (slot_of[:, None] == ids[None, :]) & (arrived[:, None] > 0)
    table = jnp.sum(jnp.where(hit, ids[:, None] + 1, 0), axis=0) - 1

    def place(along, near_part, own_part, far_part, out):
        block = (samples, LANE) if along == 1 else (LANE, width)
        return pl.pallas_call(
            functools.partial(place_kernel, edge, along),
            in_specs=[scalars(), scalars(), whole(), whole(), whole()],
            out_specs=pl.BlockSpec(memory_space=pl.ANY),
            out_shape=out,
            scratch_shapes=[pltpu.VMEM(block, jnp.float32), pltpu.SemaphoreType.DMA((slots,))],
            compiler_params=pltpu.CompilerParams(vmem_limit_bytes=24 << 20),
            name="place",
        )(table, parity, near_part, own_part, far_part)

    design_out = place(1, near_in, design, far_in, f32(samples, slots * LANE))
    coef_out = place(0, near_coef, coef_two, far_coef, f32(slots * LANE, width))
    return (coef_out, design_out, duality_gap, dual_value, mass)


def solution(mesh):
    placed = (
        P("groups", "feat"),
        P("groups", None),
        P(("groups", "feat"), None),
        P(("groups", "feat"), None),
        P("groups"),
        P(("groups", "feat")),
        P(("groups", "feat")),
    )
    return jax.shard_map(
        local,
        mesh=mesh,
        in_specs=placed,
        out_specs=(
            P(("groups", "feat"), None),
            P("groups", "feat"),
            P("groups"),
            P("groups"),
            P("groups"),
        ),
        check_vma=False,
    )
```

```python
import functools
import math

import jax
import jax.numpy as jnp
from jax import lax
from jax.experimental import pallas as pl
from jax.experimental.pallas import tpu as pltpu
from jax.sharding import PartitionSpec as P


START = 40
LANE = 128
AXIS = "feat"


def swap(value, bit):
    count = lax.axis_size(AXIS)
    return lax.ppermute(value, AXIS, [(i, i ^ bit) for i in range(count)])


def stages(count):
    return [1 << s for s in range(count.bit_length() - 1)]


def halves(values):
    high = values.astype(jnp.bfloat16)
    low = (values - high.astype(jnp.float32)).astype(jnp.bfloat16)
    return high, low


def mul(left, right):
    return lax.dot_general(left, right, (((1,), (0,)), ((), ())), preferred_element_type=jnp.float32)


def shrink(values, level):
    return values - jnp.clip(values, -level, level)


def forward(high, low, point):
    width = point.shape[1]
    ph, plo = halves(point)
    both = mul(high, jnp.concatenate([ph, plo], axis=1))
    return both[:, :width] + both[:, width:] + mul(low, ph)


def backward(high, low, turned):
    width = turned.shape[0] // 2
    both = mul(turned, high)
    return both[:width] + both[width:] + mul(turned[:width], low)


def hand_over(parity, total, keep_ref, send_ref):
    half = keep_ref.shape[0]
    keep_ref[...] = total[pl.ds(pl.multiple_of(parity * half, 8), half), :]
    send_ref[...] = total[pl.ds(pl.multiple_of((1 - parity) * half, 8), half), :]


def take_over(parity, own_ref, other_ref, targets_ref, turned, whole):
    half = own_ref.shape[0]
    whole[pl.ds(pl.multiple_of(parity * half, 8), half), :] = own_ref[...]
    whole[pl.ds(pl.multiple_of((1 - parity) * half, 8), half), :] = other_ref[...]
    width = targets_ref.shape[1]
    misfit = whole[...] - targets_ref[...]
    across = misfit.T
    high, low = halves(across)
    turned[:width] = high
    turned[width:] = low
    return misfit


def mask_of(drop_ref, dest_ref, start, count, shard):
    mask = jnp.int32(0)
    for k in range(count):
        moves = (drop_ref[start + k] == 0) & (dest_ref[start + k] == shard)
        mask = mask + jnp.where(moves, jnp.int32(1 << k), jnp.int32(0))
    return mask


def first_kernel(
    push, shards, me_ref, drop_ref, dest_ref, design_ref, now_ref, prev_ref,
    keep_ref, send_ref, near_ref, far_a_ref, far_b_ref, total,
):
    step = pl.program_id(0)
    last = pl.num_programs(0) - 1
    me = me_ref[0]
    parity = me & 1
    block = design_ref[...]
    high, low = halves(block)
    now = now_ref[...]
    part = forward(high, low, now + push * (now - prev_ref[...]))
    rows = block.shape[0]
    edge = block.shape[1] // LANE
    blocks = drop_ref.shape[0]

    @pl.when(step == 0)
    def _():
        total[...] = part

    @pl.when(step > 0)
    def _():
        total[...] += part

    def flags(ref, right):
        if right:
            mask = mask_of(drop_ref, dest_ref, blocks - edge, edge, lax.rem(me + 1, shards))
        else:
            mask = mask_of(drop_ref, dest_ref, 0, edge, lax.rem(me + shards - 1, shards))
        size = ref.shape[0]
        ref[size - 8 :, :] = jnp.full((8, ref.shape[1]), mask.astype(jnp.float32), jnp.float32)

    def put_near(right):
        near_ref[:rows, :] = block
        flags(near_ref, right)

    def put_far(right):
        far_a_ref[: rows // 2, :] = block[: rows // 2]
        far_b_ref[...] = block[rows // 2 :]
        flags(far_a_ref, right)

    @pl.when((step == 0) & (parity == 1))
    def _():
        put_near(False)

    @pl.when((step == 0) & (parity == 0))
    def _():
        put_far(False)

    @pl.when((step == last) & (parity == 0))
    def _():
        put_near(True)

    @pl.when((step == last) & (parity == 1))
    def _():
        put_far(True)

    @pl.when(step == last)
    def _():
        hand_over(parity, total, keep_ref, send_ref)


def descend_kernel(
    push_in, push_out, scale, level_scale, parity_ref, design_ref, later_ref, early_ref, own_ref, other_ref, targets_ref,
    penalty_ref, coef_ref, keep_ref, send_ref, *rest,
):
    total, turned = rest[-2:]
    step = pl.program_id(0)
    last = pl.num_programs(0) - 1
    parity = parity_ref[0] & 1

    @pl.when(step == 0)
    def _():
        take_over(parity, own_ref, other_ref, targets_ref, turned, total)

    high, low = halves(design_ref[...])
    turn = backward(high, low, turned[...])
    later = later_ref[...]
    point = later + push_in * (later - early_ref[...])
    coef = shrink(point - turn.T * (1.0 / scale), penalty_ref[...] * level_scale)
    coef_ref[...] = coef
    if push_out is not None:
        part = forward(high, low, coef + push_out * (coef - later))
    else:
        part = forward(high, low, coef)
        mass_ref, near_ref, far_ref = rest[:3]
        mass = jnp.sum(jnp.abs(coef), axis=0, keepdims=True)

        @pl.when(step == 0)
        def _():
            mass_ref[...] = mass

        @pl.when(step > 0)
        def _():
            mass_ref[...] += mass

        @pl.when(((step == 0) & (parity == 1)) | ((step == last) & (parity == 0)))
        def _():
            near_ref[...] = coef

        @pl.when(((step == 0) & (parity == 0)) | ((step == last) & (parity == 1)))
        def _():
            far_ref[...] = coef

    @pl.when(step == 0)
    def _():
        total[...] = part

    @pl.when(step > 0)
    def _():
        total[...] += part

    @pl.when(step == last)
    def _():
        hand_over(parity, total, keep_ref, send_ref)


def peak_kernel(
    parity_ref, design_ref, own_ref, other_ref, targets_ref, mass_ref,
    peak_ref, square_ref, cross_ref, total, turned, best,
):
    step = pl.program_id(0)
    parity = parity_ref[0] & 1

    @pl.when(step == 0)
    def _():
        residual = -take_over(parity, own_ref, other_ref, targets_ref, turned, total)
        square_ref[...] = jnp.sum(residual * residual, axis=0, keepdims=True)
        cross_ref[...] = jnp.sum(residual * targets_ref[...], axis=0, keepdims=True)
        best[...] = jnp.zeros_like(best)

    high, low = halves(design_ref[...])
    turn = jnp.abs(backward(high, low, turned[...]))
    for k in range(turn.shape[1] // LANE):
        best[...] = jnp.maximum(best[...], turn[:, k * LANE : (k + 1) * LANE])

    @pl.when(step == pl.num_programs(0) - 1)
    def _():
        half = peak_ref.shape[0] // 2
        peak_ref[:half] = jnp.broadcast_to(jnp.max(best[...].T, axis=0, keepdims=True), (half, LANE))
        peak_ref[half:] = jnp.broadcast_to(mass_ref[...], (half, LANE))


def place_design_kernel(
    me_ref, drop_ref, dest_ref, near_ref, own_ref, far_a_ref, far_b_ref, out_ref, table_ref, blank, sems, more,
):
    blocks = drop_ref.shape[0]
    slots = table_ref.shape[0]
    edge = (slots - blocks) // 2
    rows = out_ref.shape[0]
    half = rows // 2
    me = me_ref[0]
    parity = me & 1
    near = jnp.max(near_ref[rows:, :LANE]).astype(jnp.int32)
    far = jnp.max(far_a_ref[half:, :LANE]).astype(jnp.int32)
    before = jnp.where(parity == 1, near, far)
    after = jnp.where(parity == 1, far, near)
    blank[...] = jnp.zeros_like(blank)

    def cols(ref, index):
        return ref.at[:, pl.ds(pl.multiple_of(index * LANE, LANE), LANE)]

    def cut(ref, first, count, index):
        return ref.at[first : first + count, pl.ds(pl.multiple_of(index * LANE, LANE), LANE)]

    def from_near(slot, index):
        pltpu.make_async_copy(cut(near_ref, 0, rows, index), cols(out_ref, slot), sems.at[slot]).start()
        return jnp.int32(0)

    def from_far(slot, index):
        pltpu.make_async_copy(cut(far_a_ref, 0, half, index), cut(out_ref, 0, half, slot), more.at[0, slot]).start()
        pltpu.make_async_copy(cut(far_b_ref, 0, half, index), cut(out_ref, half, half, slot), more.at[1, slot]).start()

    count = jnp.int32(0)
    for slot in range(slots):
        table_ref[slot] = jnp.int32(-1)
    for cand in range(slots):
        if cand < edge:
            here = (before >> cand) & 1
        elif cand < edge + blocks:
            k = cand - edge
            here = jnp.where((drop_ref[k] == 0) & (dest_ref[k] == me), jnp.int32(1), jnp.int32(0))
        else:
            here = (after >> (cand - edge - blocks)) & 1

        @pl.when(here == 1)
        def _(cand=cand, count=count):
            table_ref[count] = jnp.int32(cand)

        count = count + here

    def parts(slot):
        source = table_ref[slot]
        left = (source >= 0) & (source < edge)
        right = source >= edge + blocks
        inner = jnp.where(left, source, source - edge - blocks)
        near_side = (left & (parity == 1)) | (right & (parity == 0))
        far_side = (left & (parity == 0)) | (right & (parity == 1))
        return source, inner, near_side, far_side

    for slot in range(slots):
        source, inner, near_side, far_side = parts(slot)

        @pl.when(source < 0)
        def _(slot=slot):
            pltpu.make_async_copy(blank, cols(out_ref, slot), sems.at[slot]).start()

        @pl.when((source >= edge) & (source < edge + blocks))
        def _(slot=slot, source=source):
            pltpu.make_async_copy(cols(own_ref, source - edge), cols(out_ref, slot), sems.at[slot]).start()

        @pl.when(near_side)
        def _(slot=slot, inner=inner):
            from_near(slot, inner)

        @pl.when(far_side)
        def _(slot=slot, inner=inner):
            from_far(slot, inner)

    for slot in range(slots):
        far_side = parts(slot)[3]

        @pl.when(far_side)
        def _(slot=slot):
            for part, ref in enumerate((far_a_ref, far_b_ref)):
                pltpu.make_async_copy(cut(ref, 0, half, 0), cut(out_ref, part * half, half, slot), more.at[part, slot]).wait()

        @pl.when(jnp.logical_not(far_side))
        def _(slot=slot):
            pltpu.make_async_copy(blank, cols(out_ref, slot), sems.at[slot]).wait()


def place_coef_kernel(edge, me_ref, table_ref, near_ref, own_ref, far_ref, out_ref, blank, sems):
    slots = table_ref.shape[0]
    own = slots - 2 * edge
    parity = me_ref[0] & 1
    blank[...] = jnp.zeros_like(blank)

    def rows(ref, index):
        return ref.at[pl.ds(pl.multiple_of(index * LANE, LANE), LANE), :]

    def copy(slot, src):
        return pltpu.make_async_copy(src, rows(out_ref, slot), sems.at[slot])

    for slot in range(slots):
        source = table_ref[slot]
        left = (source >= 0) & (source < edge)
        right = source >= edge + own
        inner = jnp.where(left, source, source - edge - own)

        @pl.when(source < 0)
        def _(slot=slot):
            copy(slot, blank).start()

        @pl.when((source >= edge) & (source < edge + own))
        def _(slot=slot, source=source):
            copy(slot, rows(own_ref, source - edge)).start()

        @pl.when((left & (parity == 1)) | (right & (parity == 0)))
        def _(slot=slot, inner=inner):
            copy(slot, rows(near_ref, inner)).start()

        @pl.when((left & (parity == 0)) | (right & (parity == 1)))
        def _(slot=slot, inner=inner):
            copy(slot, rows(far_ref, inner)).start()

    for slot in range(slots):
        copy(slot, blank).wait()


VM = pltpu.MemorySpace.VMEM
SM = pltpu.MemorySpace.SMEM


def whole():
    return pl.BlockSpec(memory_space=VM)


def scalars():
    return pl.BlockSpec(memory_space=SM)


def f32(*shape):
    return jax.ShapeDtypeStruct(shape, jnp.float32)


def fixed(shape):
    return pl.BlockSpec(shape, lambda i: (0,) * len(shape))


def body(design, targets, coef_now, coef_prev, penalty, drop_mask, dest_shard):
    samples, feats = design.shape
    width = targets.shape[1]
    shards = lax.axis_size(AXIS)
    me = lax.axis_index(AXIS).astype(jnp.int32).reshape(1)
    lipschitz = (math.sqrt(samples) + math.sqrt(feats * shards)) ** 2
    first_push = (START - 1) / (START + 2)
    second_push = START / (START + 3)
    blocks = feats // LANE
    edge = blocks // 4
    slots = blocks + 2 * edge
    chunk = edge * LANE
    steps = feats // chunk
    half = samples // 2
    bits = stages(shards)

    def feat_spec():
        return pl.BlockSpec((samples, chunk), lambda i: (0, i))

    def coef_spec():
        return pl.BlockSpec((chunk, width), lambda i: (i, 0))

    params = pltpu.CompilerParams(vmem_limit_bytes=24 << 20, dimension_semantics=("arbitrary",))
    row_spec = fixed((1, width))
    half_spec = fixed((half, width))
    line = penalty.reshape(1, width)

    def in_hbm(value):
        return pltpu.with_memory_space_constraint(value, pltpu.MemorySpace.HBM)

    drop, dest = in_hbm(drop_mask), in_hbm(dest_shard)
    edge_shapes = [(samples + 8, chunk), (half + 8, chunk), (half, chunk)]
    keep, send, near, far_a, far_b = pl.pallas_call(
        functools.partial(first_kernel, first_push, shards),
        grid=(steps,),
        in_specs=[scalars(), scalars(), scalars(), feat_spec(), coef_spec(), coef_spec()],
        out_specs=[half_spec, half_spec] + [fixed(shape) for shape in edge_shapes],
        out_shape=[f32(half, width)] * 2 + [f32(*shape) for shape in edge_shapes],
        scratch_shapes=[pltpu.VMEM((samples, width), jnp.float32)],
        compiler_params=params,
        name="first",
    )(me, drop, dest, in_hbm(design), in_hbm(coef_now), in_hbm(coef_prev))

    def inward(value):
        return swap(value, 1)

    def outward(value):
        pairs = [(i, (i + 1) % shards if i % 2 else (i - 1) % shards) for i in range(shards)]
        return lax.ppermute(value, AXIS, pairs)

    def combine(keep, send):
        total = keep + swap(send, 1)
        for bit in bits[1:]:
            total = total + swap(total, bit)
        other = swap(total, 1)
        return total, other

    near_in = inward(near)
    far_a_in = outward(far_a)
    far_b_in = outward(far_b)

    turned = pltpu.VMEM((2 * width, samples), jnp.bfloat16)
    sum_scratch = pltpu.VMEM((samples, width), jnp.float32)

    def descend(push_in, push_out, later, early, own, other):
        out_specs = [coef_spec(), half_spec, half_spec]
        out_shape = [f32(feats, width), f32(half, width), f32(half, width)]
        if push_out is None:
            out_specs += [row_spec, fixed((chunk, width)), fixed((chunk, width))]
            out_shape += [f32(1, width), f32(chunk, width), f32(chunk, width)]
        return pl.pallas_call(
            functools.partial(descend_kernel, push_in, push_out, lipschitz, samples / lipschitz),
            grid=(steps,),
            in_specs=[scalars(), feat_spec(), coef_spec(), coef_spec(), half_spec, half_spec, fixed((samples, width)), row_spec],
            out_specs=out_specs,
            out_shape=out_shape,
            scratch_shapes=[sum_scratch, turned],
            compiler_params=params,
            name="descend",
        )(me, design, later, early, own, other, targets, line)

    own, other = combine(keep, send)
    coef_one, keep, send = descend(first_push, second_push, coef_now, coef_prev, own, other)
    own, other = combine(keep, send)
    coef_two, keep, send, mass, near, far = descend(second_push, None, coef_one, coef_now, own, other)
    near_coef = inward(near)
    far_coef = outward(far)
    own, other = combine(keep, send)

    design_out, table = pl.pallas_call(
        place_design_kernel,
        in_specs=[scalars(), scalars(), scalars(), whole(), whole(), whole(), whole()],
        out_specs=[pl.BlockSpec(memory_space=pl.ANY), scalars()],
        out_shape=[f32(samples, slots * LANE), jax.ShapeDtypeStruct((slots,), jnp.int32)],
        scratch_shapes=[
            pltpu.VMEM((samples, LANE), jnp.float32),
            pltpu.SemaphoreType.DMA((slots,)),
            pltpu.SemaphoreType.DMA((2, slots)),
        ],
        compiler_params=pltpu.CompilerParams(vmem_limit_bytes=24 << 20),
        name="place_design",
    )(me, drop, dest, near_in, design, far_a_in, far_b_in)

    tail, square, cross = pl.pallas_call(
        peak_kernel,
        grid=(steps,),
        in_specs=[scalars(), feat_spec(), half_spec, half_spec, fixed((samples, width)), row_spec],
        out_specs=[fixed((16, width)), row_spec, row_spec],
        out_shape=[f32(16, width), f32(1, width), f32(1, width)],
        scratch_shapes=[sum_scratch, turned, pltpu.VMEM((width, LANE), jnp.float32)],
        compiler_params=params,
        name="peak",
    )(me, design, own, other, targets, mass)
    is_peak = lax.broadcasted_iota(jnp.int32, (16, width), 0) < 8
    for bit in bits:
        got = swap(tail, bit)
        tail = jnp.where(is_peak, jnp.maximum(tail, got), tail + got)

    coef_out = pl.pallas_call(
        functools.partial(place_coef_kernel, edge),
        in_specs=[scalars(), scalars(), whole(), whole(), whole()],
        out_specs=pl.BlockSpec(memory_space=pl.ANY),
        out_shape=f32(slots * LANE, width),
        scratch_shapes=[pltpu.VMEM((LANE, width), jnp.float32), pltpu.SemaphoreType.DMA((slots,))],
        compiler_params=pltpu.CompilerParams(vmem_limit_bytes=24 << 20),
        name="place_coef",
    )(me, table, near_coef, coef_two, far_coef)

    peak, mass = tail[0], tail[8]
    dual_scale = jnp.maximum(penalty, peak / samples)
    ratio = penalty / dual_scale
    dual_value = (2.0 * ratio * cross[0] - ratio * ratio * square[0]) / (2.0 * samples)
    duality_gap = square[0] / (2.0 * samples) + penalty * mass - dual_value
    return (coef_out, design_out, duality_gap, dual_value, mass)


def solution(mesh):
    placed = (
        P("groups", "feat"),
        P("groups", None),
        P(("groups", "feat"), None),
        P(("groups", "feat"), None),
        P("groups"),
        P(("groups", "feat")),
        P(("groups", "feat")),
    )
    return jax.shard_map(
        body,
        mesh=mesh,
        in_specs=placed,
        out_specs=(
            P(("groups", "feat"), None),
            P("groups", "feat"),
            P("groups"),
            P("groups"),
            P("groups"),
        ),
        check_vma=False,
    )
```

```python
import functools
import math

import jax
import jax.numpy as jnp
from jax import lax
from jax.experimental import pallas as pl
from jax.experimental.pallas import tpu as pltpu
from jax.sharding import PartitionSpec as P


START = 40
LANE = 128
AXIS = "feat"


def swap(value, bit):
    count = lax.axis_size(AXIS)
    return lax.ppermute(value, AXIS, [(i, i ^ bit) for i in range(count)])


def stages(count):
    return [1 << s for s in range(count.bit_length() - 1)]


def halves(values):
    high = values.astype(jnp.bfloat16)
    low = (values - high.astype(jnp.float32)).astype(jnp.bfloat16)
    return high, low


def mul(left, right):
    return lax.dot_general(left, right, (((1,), (0,)), ((), ())), preferred_element_type=jnp.float32)


def shrink(values, level):
    return values - jnp.clip(values, -level, level)


def forward(high, low, point):
    width = point.shape[1]
    ph, plo = halves(point)
    both = mul(high, jnp.concatenate([ph, plo], axis=1))
    return both[:, :width] + both[:, width:] + mul(low, ph)


def backward(high, low, turned):
    width = turned.shape[0] // 2
    both = mul(turned, high)
    return both[:width] + both[width:] + mul(turned[:width], low)


def hand_over(parity, total, keep_ref, send_ref):
    half = keep_ref.shape[0]
    keep_ref[...] = total[pl.ds(pl.multiple_of(parity * half, 8), half), :]
    send_ref[...] = total[pl.ds(pl.multiple_of((1 - parity) * half, 8), half), :]


def take_over(parity, own_ref, other_ref, targets_ref, whole):
    half = own_ref.shape[0]
    whole[pl.ds(pl.multiple_of(parity * half, 8), half), :] = own_ref[...]
    whole[pl.ds(pl.multiple_of((1 - parity) * half, 8), half), :] = other_ref[...]
    misfit = whole[...] - targets_ref[...]
    high, low = halves(misfit.T)
    return misfit, jnp.concatenate([high, low], axis=0)


def mask_of(drop_ref, dest_ref, start, count, shard):
    mask = jnp.int32(0)
    for k in range(count):
        moves = (drop_ref[start + k] == 0) & (dest_ref[start + k] == shard)
        mask = mask + jnp.where(moves, jnp.int32(1 << k), jnp.int32(0))
    return mask


def first_kernel(
    push, shards, chunk, me_ref, drop_ref, dest_ref, design_ref, now_ref, prev_ref,
    keep_ref, send_ref, near_ref, far_a_ref, far_b_ref, held_ref, high_ref, low_ref, base_ref, point_ref,
    prev, total, sems,
):
    me = me_ref[0]
    parity = me & 1
    rows, feats = design_ref.shape
    blocks = drop_ref.shape[0]
    edge = chunk // LANE
    steps = feats // chunk

    def copies(step):
        part = pl.ds(step * chunk, chunk)
        return [
            pltpu.make_async_copy(design_ref.at[:, part], held_ref.at[:, part], sems.at[0, step]),
            pltpu.make_async_copy(now_ref.at[part, :], base_ref.at[part, :], sems.at[1, step]),
            pltpu.make_async_copy(prev_ref.at[part, :], prev.at[part, :], sems.at[2, step]),
        ]

    for step in range(steps):
        for copy in copies(step):
            copy.start()
    for step in range(steps):
        for copy in copies(step):
            copy.wait()
        part = slice(step * chunk, (step + 1) * chunk)
        high, low = halves(held_ref[:, part])
        high_ref[:, part] = high
        low_ref[:, part] = low
        now = base_ref[part, :]
        point = now + push * (now - prev[part, :])
        point_ref[part, :] = point
        ahead = forward(high, low, point)
        if step == 0:
            total[...] = ahead
        else:
            total[...] += ahead
    hand_over(parity, total, keep_ref, send_ref)

    def put(right, near):
        block = held_ref[:, feats - chunk :] if right else held_ref[:, :chunk]
        if right:
            mask = mask_of(drop_ref, dest_ref, blocks - edge, edge, lax.rem(me + 1, shards))
        else:
            mask = mask_of(drop_ref, dest_ref, 0, edge, lax.rem(me + shards - 1, shards))
        ref = near_ref if near else far_a_ref
        if near:
            near_ref[:rows, :] = block
        else:
            far_a_ref[: rows // 2, :] = block[: rows // 2]
            far_b_ref[...] = block[rows // 2 :]
        ref[ref.shape[0] - 8 :, :] = jnp.full((8, chunk), mask.astype(jnp.float32), jnp.float32)

    @pl.when(parity == 1)
    def _():
        put(False, True)
        put(True, False)

    @pl.when(parity == 0)
    def _():
        put(True, True)
        put(False, False)


def descend_kernel(
    ahead, chunk, scale, level_scale, me_ref, high_ref, low_ref, point_ref, base_ref, own_ref, other_ref, targets_ref,
    penalty_ref, coef_ref, keep_ref, send_ref, *rest,
):
    total, split = rest[-2:]
    parity = me_ref[0] & 1
    _, feats = high_ref.shape
    width = targets_ref.shape[1]
    _, turned = take_over(parity, own_ref, other_ref, targets_ref, total)
    level = penalty_ref[...] * level_scale
    mass = jnp.zeros((1, width), jnp.float32)
    for step in range(feats // chunk):
        part = slice(step * chunk, (step + 1) * chunk)
        turn = backward(high_ref[:, part], low_ref[:, part], turned)
        coef = shrink(point_ref[part, :] - turn.T * (1.0 / scale), level)
        coef_ref[part, :] = coef
        if ahead is not None:
            coef = coef + ahead * (coef - base_ref[part, :])
            rest[0][part, :] = coef
        else:
            mass = mass + jnp.sum(jnp.abs(coef), axis=0, keepdims=True)
        ph, plo = halves(coef)
        split[part, :width] = ph
        split[part, width:] = plo
    both = mul(high_ref[...], split[...])
    total[...] = both[:, :width] + both[:, width:] + mul(low_ref[...], split[:, :width])
    hand_over(parity, total, keep_ref, send_ref)
    if ahead is None:
        mass_ref, near_ref, far_ref = rest[:3]
        mass_ref[...] = mass

        @pl.when(parity == 1)
        def _():
            near_ref[...] = coef_ref[: near_ref.shape[0], :]
            far_ref[...] = coef_ref[feats - far_ref.shape[0] :, :]

        @pl.when(parity == 0)
        def _():
            far_ref[...] = coef_ref[: far_ref.shape[0], :]
            near_ref[...] = coef_ref[feats - near_ref.shape[0] :, :]


def peak_kernel(
    chunk, me_ref, high_ref, low_ref, own_ref, other_ref, targets_ref, mass_ref, peak_ref, square_ref, cross_ref, total,
):
    parity = me_ref[0] & 1
    misfit, turned = take_over(parity, own_ref, other_ref, targets_ref, total)
    square_ref[...] = jnp.sum(misfit * misfit, axis=0, keepdims=True)
    cross_ref[...] = -jnp.sum(misfit * targets_ref[...], axis=0, keepdims=True)
    best = None
    for step in range(high_ref.shape[1] // chunk):
        part = slice(step * chunk, (step + 1) * chunk)
        turn = jnp.abs(backward(high_ref[:, part], low_ref[:, part], turned))
        for k in range(chunk // LANE):
            piece = turn[:, k * LANE : (k + 1) * LANE]
            best = piece if best is None else jnp.maximum(best, piece)
    half = peak_ref.shape[0] // 2
    peak_ref[:half] = jnp.broadcast_to(jnp.max(best.T, axis=0, keepdims=True), (half, LANE))
    peak_ref[half:] = jnp.broadcast_to(mass_ref[...], (half, LANE))


def cols(ref, index):
    return ref.at[:, pl.ds(pl.multiple_of(index * LANE, LANE), LANE)]


def cut(ref, first, count, index):
    return ref.at[first : first + count, pl.ds(pl.multiple_of(index * LANE, LANE), LANE)]


def sides(source, edge, blocks, parity):
    left = (source >= 0) & (source < edge)
    right = source >= edge + blocks
    inner = jnp.where(left, source, source - edge - blocks)
    near_side = (left & (parity == 1)) | (right & (parity == 0))
    far_side = (left & (parity == 0)) | (right & (parity == 1))
    return inner, near_side, far_side


def tabulate(me_ref, drop_ref, dest_ref, near_ref, far_ref, table_ref):
    blocks = drop_ref.shape[0]
    slots = table_ref.shape[0]
    edge = (slots - blocks) // 2
    me = me_ref[0]
    near = jnp.max(near_ref[near_ref.shape[0] - 8 :, :LANE]).astype(jnp.int32)
    far = jnp.max(far_ref[far_ref.shape[0] - 8 :, :LANE]).astype(jnp.int32)
    before = jnp.where((me & 1) == 1, near, far)
    after = jnp.where((me & 1) == 1, far, near)
    for slot in range(slots):
        table_ref[slot] = jnp.int32(-1)
    count = jnp.int32(0)
    for cand in range(slots):
        if cand < edge:
            here = (before >> cand) & 1
        elif cand < edge + blocks:
            k = cand - edge
            here = jnp.where((drop_ref[k] == 0) & (dest_ref[k] == me), jnp.int32(1), jnp.int32(0))
        else:
            here = (after >> (cand - edge - blocks)) & 1

        @pl.when(here == 1)
        def _(cand=cand, count=count):
            table_ref[count] = jnp.int32(cand)

        count = count + here


def place_own(first, last, edge, blocks, parity, table_ref, near_ref, own_ref, out_ref, blank, sems):
    rows = out_ref.shape[0]
    blank[...] = jnp.zeros_like(blank)
    for slot in range(first, last):
        source = table_ref[slot]
        inner, near_side, _ = sides(source, edge, blocks, parity)

        @pl.when(source < 0)
        def _(slot=slot):
            pltpu.make_async_copy(blank, cols(out_ref, slot), sems.at[slot]).start()

        @pl.when((source >= edge) & (source < edge + blocks))
        def _(slot=slot, source=source):
            pltpu.make_async_copy(cols(own_ref, source - edge), cols(out_ref, slot), sems.at[slot]).start()

        @pl.when(near_side)
        def _(slot=slot, inner=inner):
            pltpu.make_async_copy(cut(near_ref, 0, rows, inner), cols(out_ref, slot), sems.at[slot]).start()

    for slot in range(first, last):
        far_side = sides(table_ref[slot], edge, blocks, parity)[2]

        @pl.when(jnp.logical_not(far_side))
        def _(slot=slot):
            pltpu.make_async_copy(blank, cols(out_ref, slot), sems.at[slot]).wait()


def place_a_kernel(me_ref, drop_ref, dest_ref, near_ref, far_ref, own_ref, out_ref, table_ref, blank, sems):
    slots = table_ref.shape[0]
    blocks = drop_ref.shape[0]
    tabulate(me_ref, drop_ref, dest_ref, near_ref, far_ref, table_ref)
    place_own(0, slots // 2, (slots - blocks) // 2, blocks, me_ref[0] & 1, table_ref, near_ref, own_ref, out_ref, blank, sems)


def place_b_kernel(edge, me_ref, table_ref, near_ref, own_ref, given_ref, out_ref, blank, sems):
    slots = table_ref.shape[0]
    place_own(slots // 2, slots, edge, slots - 2 * edge, me_ref[0] & 1, table_ref, near_ref, own_ref, out_ref, blank, sems)


def place_c_kernel(edge, me_ref, table_ref, far_a_ref, far_b_ref, given_ref, out_ref, sems):
    slots = table_ref.shape[0]
    half = out_ref.shape[0] // 2
    parity = me_ref[0] & 1

    def each(slot, inner):
        return [
            pltpu.make_async_copy(cut(ref, 0, half, inner), cut(out_ref, k * half, half, slot), sems.at[k, slot])
            for k, ref in enumerate((far_a_ref, far_b_ref))
        ]

    for slot in range(slots):
        inner, _, far_side = sides(table_ref[slot], edge, slots - 2 * edge, parity)

        @pl.when(far_side)
        def _(slot=slot, inner=inner):
            for copy in each(slot, inner):
                copy.start()

    for slot in range(slots):
        far_side = sides(table_ref[slot], edge, slots - 2 * edge, parity)[2]

        @pl.when(far_side)
        def _(slot=slot):
            for copy in each(slot, 0):
                copy.wait()


def place_coef_kernel(edge, me_ref, table_ref, near_ref, own_ref, far_ref, out_ref, blank, sems):
    slots = table_ref.shape[0]
    own = slots - 2 * edge
    parity = me_ref[0] & 1
    blank[...] = jnp.zeros_like(blank)

    def rows(ref, index):
        return ref.at[pl.ds(pl.multiple_of(index * LANE, LANE), LANE), :]

    def copy(slot, src):
        return pltpu.make_async_copy(src, rows(out_ref, slot), sems.at[slot])

    for slot in range(slots):
        source = table_ref[slot]
        left = (source >= 0) & (source < edge)
        right = source >= edge + own
        inner = jnp.where(left, source, source - edge - own)

        @pl.when(source < 0)
        def _(slot=slot):
            copy(slot, blank).start()

        @pl.when((source >= edge) & (source < edge + own))
        def _(slot=slot, source=source):
            copy(slot, rows(own_ref, source - edge)).start()

        @pl.when((left & (parity == 1)) | (right & (parity == 0)))
        def _(slot=slot, inner=inner):
            copy(slot, rows(near_ref, inner)).start()

        @pl.when((left & (parity == 0)) | (right & (parity == 1)))
        def _(slot=slot, inner=inner):
            copy(slot, rows(far_ref, inner)).start()

    for slot in range(slots):
        copy(slot, blank).wait()


VM = pltpu.MemorySpace.VMEM
SM = pltpu.MemorySpace.SMEM


def whole():
    return pl.BlockSpec(memory_space=VM)


def scalars():
    return pl.BlockSpec(memory_space=SM)


def f32(*shape):
    return jax.ShapeDtypeStruct(shape, jnp.float32)


def body(design, targets, coef_now, coef_prev, penalty, drop_mask, dest_shard):
    samples, feats = design.shape
    width = targets.shape[1]
    shards = lax.axis_size(AXIS)
    me = lax.axis_index(AXIS).astype(jnp.int32).reshape(1)
    lipschitz = (math.sqrt(samples) + math.sqrt(feats * shards)) ** 2
    first_push = (START - 1) / (START + 2)
    second_push = START / (START + 3)
    blocks = feats // LANE
    edge = blocks // 4
    slots = blocks + 2 * edge
    chunk = edge * LANE
    steps = feats // chunk
    half = samples // 2
    bits = stages(shards)

    params = pltpu.CompilerParams(vmem_limit_bytes=24 << 20)
    line = penalty.reshape(1, width)
    anywhere = pl.BlockSpec(memory_space=pl.ANY)

    def in_hbm(value):
        return pltpu.with_memory_space_constraint(value, pltpu.MemorySpace.HBM)

    def b16(*shape):
        return jax.ShapeDtypeStruct(shape, jnp.bfloat16)

    drop, dest = in_hbm(drop_mask), in_hbm(dest_shard)
    keep, send, near, far_a, far_b, held, high, low, base, point = pl.pallas_call(
        functools.partial(first_kernel, first_push, shards, chunk),
        in_specs=[scalars()] * 3 + [anywhere] * 3,
        out_specs=[whole()] * 10,
        out_shape=[
            f32(half, width), f32(half, width), f32(samples + 8, chunk), f32(half + 8, chunk), f32(half, chunk),
            f32(samples, feats), b16(samples, feats), b16(samples, feats), f32(feats, width), f32(feats, width),
        ],
        scratch_shapes=[
            pltpu.VMEM((feats, width), jnp.float32),
            pltpu.VMEM((samples, width), jnp.float32),
            pltpu.SemaphoreType.DMA((3, steps)),
        ],
        compiler_params=params,
        name="first",
    )(me, drop, dest, in_hbm(design), in_hbm(coef_now), in_hbm(coef_prev))

    def inward(value):
        return swap(value, 1)

    def outward(value):
        pairs = [(i, (i + 1) % shards if i % 2 else (i - 1) % shards) for i in range(shards)]
        return lax.ppermute(value, AXIS, pairs)

    even_bits = bits[-1:] + bits[1:-1]
    odd_bits = bits[2:] + bits[1:2]

    def combine(keep, send):
        total = keep + swap(send, 1)
        for even, odd in zip(even_bits, odd_bits):
            pairs = [(i, i ^ (odd if i % 2 else even)) for i in range(shards)]
            total = total + lax.ppermute(total, AXIS, pairs)
        other = swap(total, 1)
        return total, other

    near_in = inward(near)
    far_a_in = outward(far_a)
    far_b_in = outward(far_b)

    sum_scratch = pltpu.VMEM((samples, width), jnp.float32)

    def descend(ahead, point, base, own, other):
        out_shape = [f32(feats, width), f32(half, width), f32(half, width)]
        if ahead is None:
            out_shape += [f32(1, width), f32(chunk, width), f32(chunk, width)]
        else:
            out_shape += [f32(feats, width)]
        return pl.pallas_call(
            functools.partial(descend_kernel, ahead, chunk, lipschitz, samples / lipschitz),
            in_specs=[scalars()] + [whole()] * 8,
            out_specs=[whole()] * len(out_shape),
            out_shape=out_shape,
            scratch_shapes=[sum_scratch, pltpu.VMEM((feats, 2 * width), jnp.bfloat16)],
            compiler_params=params,
            name="descend",
        )(me, high, low, point, base, own, other, targets, line)

    own, other = combine(keep, send)
    coef_one, keep, send, point = descend(second_push, point, base, own, other)
    own, other = combine(keep, send)
    coef_two, keep, send, mass, near, far = descend(None, point, coef_one, own, other)
    near_coef = inward(near)
    far_coef = outward(far)
    own, other = combine(keep, send)

    blank = pltpu.VMEM((samples, LANE), jnp.float32)
    out_form = f32(samples, slots * LANE)
    design_out, table = pl.pallas_call(
        place_a_kernel,
        in_specs=[scalars()] * 3 + [whole()] * 3,
        out_specs=[anywhere, scalars()],
        out_shape=[out_form, jax.ShapeDtypeStruct((slots,), jnp.int32)],
        scratch_shapes=[blank, pltpu.SemaphoreType.DMA((slots,))],
        compiler_params=params,
        name="place_a",
    )(me, drop, dest, near_in, far_a_in, held)
    design_out = pl.pallas_call(
        functools.partial(place_b_kernel, edge),
        in_specs=[scalars()] * 2 + [whole()] * 2 + [anywhere],
        out_specs=anywhere,
        out_shape=out_form,
        scratch_shapes=[blank, pltpu.SemaphoreType.DMA((slots,))],
        input_output_aliases={4: 0},
        compiler_params=params,
        name="place_b",
    )(me, table, near_in, held, design_out)
    design_out = pl.pallas_call(
        functools.partial(place_c_kernel, edge),
        in_specs=[scalars()] * 2 + [whole()] * 2 + [anywhere],
        out_specs=anywhere,
        out_shape=out_form,
        scratch_shapes=[pltpu.SemaphoreType.DMA((2, slots))],
        input_output_aliases={4: 0},
        compiler_params=params,
        name="place_c",
    )(me, table, far_a_in, far_b_in, design_out)

    tail, square, cross = pl.pallas_call(
        functools.partial(peak_kernel, chunk),
        in_specs=[scalars()] + [whole()] * 6,
        out_specs=[whole()] * 3,
        out_shape=[f32(16, width), f32(1, width), f32(1, width)],
        scratch_shapes=[sum_scratch],
        compiler_params=params,
        name="peak",
    )(me, high, low, own, other, targets, mass)
    is_peak = lax.broadcasted_iota(jnp.int32, (16, width), 0) < 8
    for bit in bits:
        got = swap(tail, bit)
        tail = jnp.where(is_peak, jnp.maximum(tail, got), tail + got)

    coef_out = pl.pallas_call(
        functools.partial(place_coef_kernel, edge),
        in_specs=[scalars(), scalars(), whole(), whole(), whole()],
        out_specs=anywhere,
        out_shape=f32(slots * LANE, width),
        scratch_shapes=[pltpu.VMEM((LANE, width), jnp.float32), pltpu.SemaphoreType.DMA((slots,))],
        compiler_params=params,
        name="place_coef",
    )(me, table, near_coef, coef_two, far_coef)

    peak, mass = tail[0], tail[8]
    dual_scale = jnp.maximum(penalty, peak / samples)
    ratio = penalty / dual_scale
    dual_value = (2.0 * ratio * cross[0] - ratio * ratio * square[0]) / (2.0 * samples)
    duality_gap = square[0] / (2.0 * samples) + penalty * mass - dual_value
    return (coef_out, design_out, duality_gap, dual_value, mass)


def solution(mesh):
    placed = (
        P("groups", "feat"),
        P("groups", None),
        P(("groups", "feat"), None),
        P(("groups", "feat"), None),
        P("groups"),
        P(("groups", "feat")),
        P(("groups", "feat")),
    )
    return jax.shard_map(
        body,
        mesh=mesh,
        in_specs=placed,
        out_specs=(
            P(("groups", "feat"), None),
            P("groups", "feat"),
            P("groups"),
            P("groups"),
            P("groups"),
        ),
        check_vma=False,
    )
```

```python
import functools
import math

import jax
import jax.numpy as jnp
from jax import lax
from jax.experimental import pallas as pl
from jax.experimental.pallas import tpu as pltpu
from jax.sharding import PartitionSpec as P


START = 40
LANE = 128
AXIS = "feat"


def swap(value, bit):
    count = lax.axis_size(AXIS)
    return lax.ppermute(value, AXIS, [(i, i ^ bit) for i in range(count)])


def stages(count):
    return [1 << s for s in range(count.bit_length() - 1)]


def halves(values):
    high = values.astype(jnp.bfloat16)
    low = (values - high.astype(jnp.float32)).astype(jnp.bfloat16)
    return high, low


def mul(left, right):
    return lax.dot_general(left, right, (((1,), (0,)), ((), ())), preferred_element_type=jnp.float32)


def shrink(values, level):
    return values - jnp.clip(values, -level, level)


def forward(high, low, point):
    width = point.shape[1]
    ph, plo = halves(point)
    both = mul(high, jnp.concatenate([ph, plo], axis=1))
    return both[:, :width] + both[:, width:] + mul(low, ph)


def backward(high, low, turned):
    width = turned.shape[0] // 2
    both = mul(turned, high)
    return both[:width] + both[width:] + mul(turned[:width], low)


def hand_over(parity, total, keep_ref, send_ref):
    half = keep_ref.shape[0]
    keep_ref[...] = total[pl.ds(pl.multiple_of(parity * half, 8), half), :]
    send_ref[...] = total[pl.ds(pl.multiple_of((1 - parity) * half, 8), half), :]


def rows_of(side, half):
    return pl.ds(pl.multiple_of(side * half, half), half)


def turned_misfit(side, sum_ref, targets_ref):
    half = sum_ref.shape[0]
    wanted = targets_ref[rows_of(side, half), :]
    misfit = sum_ref[...] - wanted
    high, low = halves(misfit.T)
    return misfit, wanted, jnp.concatenate([high, low], axis=0)


def half_kernel(chunk, me_ref, high_ref, low_ref, own_ref, targets_ref, turn_ref):
    side = me_ref[0] & 1
    _, _, turned = turned_misfit(side, own_ref, targets_ref)
    rows = rows_of(side, own_ref.shape[0])
    for step in range(high_ref.shape[1] // chunk):
        part = slice(step * chunk, (step + 1) * chunk)
        turn_ref[:, part] = backward(high_ref[rows, part], low_ref[rows, part], turned)


def mask_of(drop_ref, dest_ref, start, count, shard):
    mask = jnp.int32(0)
    for k in range(count):
        moves = (drop_ref[start + k] == 0) & (dest_ref[start + k] == shard)
        mask = mask + jnp.where(moves, jnp.int32(1 << k), jnp.int32(0))
    return mask


def first_kernel(
    push, shards, chunk, me_ref, drop_ref, dest_ref, design_ref, now_ref, prev_ref,
    keep_ref, send_ref, near_ref, far_a_ref, far_b_ref, held_ref, high_ref, low_ref, base_ref, point_ref,
    prev, total, sems,
):
    me = me_ref[0]
    parity = me & 1
    rows, feats = design_ref.shape
    blocks = drop_ref.shape[0]
    edge = chunk // LANE
    steps = feats // chunk

    def copies(step):
        part = pl.ds(step * chunk, chunk)
        return [
            pltpu.make_async_copy(design_ref.at[:, part], held_ref.at[:, part], sems.at[0, step]),
            pltpu.make_async_copy(now_ref.at[part, :], base_ref.at[part, :], sems.at[1, step]),
            pltpu.make_async_copy(prev_ref.at[part, :], prev.at[part, :], sems.at[2, step]),
        ]

    for step in range(steps):
        for copy in copies(step):
            copy.start()
    for step in range(steps):
        for copy in copies(step):
            copy.wait()
        part = slice(step * chunk, (step + 1) * chunk)
        high, low = halves(held_ref[:, part])
        high_ref[:, part] = high
        low_ref[:, part] = low
        now = base_ref[part, :]
        point = now + push * (now - prev[part, :])
        point_ref[part, :] = point
        ahead = forward(high, low, point)
        if step == 0:
            total[...] = ahead
        else:
            total[...] += ahead
    hand_over(parity, total, keep_ref, send_ref)

    def put(right, near):
        block = held_ref[:, feats - chunk :] if right else held_ref[:, :chunk]
        if right:
            mask = mask_of(drop_ref, dest_ref, blocks - edge, edge, lax.rem(me + 1, shards))
        else:
            mask = mask_of(drop_ref, dest_ref, 0, edge, lax.rem(me + shards - 1, shards))
        ref = near_ref if near else far_a_ref
        if near:
            near_ref[:rows, :] = block
        else:
            far_a_ref[: rows // 2, :] = block[: rows // 2]
            far_b_ref[...] = block[rows // 2 :]
        ref[ref.shape[0] - 8 :, :] = jnp.full((8, chunk), mask.astype(jnp.float32), jnp.float32)

    @pl.when(parity == 1)
    def _():
        put(False, True)
        put(True, False)

    @pl.when(parity == 0)
    def _():
        put(True, True)
        put(False, False)


def descend_kernel(
    ahead, chunk, scale, level_scale, me_ref, high_ref, low_ref, point_ref, base_ref, turn_ref, other_ref, targets_ref,
    penalty_ref, coef_ref, keep_ref, send_ref, *rest,
):
    total, split = rest[-2:]
    parity = me_ref[0] & 1
    _, feats = high_ref.shape
    width = targets_ref.shape[1]
    _, _, turned = turned_misfit(1 - parity, other_ref, targets_ref)
    across = rows_of(1 - parity, other_ref.shape[0])
    level = penalty_ref[...] * level_scale
    mass = jnp.zeros((1, width), jnp.float32)
    for step in range(feats // chunk):
        part = slice(step * chunk, (step + 1) * chunk)
        turn = turn_ref[:, part] + backward(high_ref[across, part], low_ref[across, part], turned)
        coef = shrink(point_ref[part, :] - turn.T * (1.0 / scale), level)
        coef_ref[part, :] = coef
        if ahead is not None:
            coef = coef + ahead * (coef - base_ref[part, :])
            rest[0][part, :] = coef
        else:
            mass = mass + jnp.sum(jnp.abs(coef), axis=0, keepdims=True)
        ph, plo = halves(coef)
        split[part, :width] = ph
        split[part, width:] = plo
    both = mul(high_ref[...], split[...])
    total[...] = both[:, :width] + both[:, width:] + mul(low_ref[...], split[:, :width])
    hand_over(parity, total, keep_ref, send_ref)
    if ahead is None:
        mass_ref, near_ref, far_ref = rest[:3]
        mass_ref[...] = mass

        @pl.when(parity == 1)
        def _():
            near_ref[...] = coef_ref[: near_ref.shape[0], :]
            far_ref[...] = coef_ref[feats - far_ref.shape[0] :, :]

        @pl.when(parity == 0)
        def _():
            far_ref[...] = coef_ref[: far_ref.shape[0], :]
            near_ref[...] = coef_ref[feats - near_ref.shape[0] :, :]


def peak_kernel(
    chunk, me_ref, high_ref, low_ref, turn_ref, own_ref, other_ref, targets_ref, mass_ref, peak_ref, square_ref, cross_ref,
):
    parity = me_ref[0] & 1
    mine, wanted, _ = turned_misfit(parity, own_ref, targets_ref)
    theirs, needed, turned = turned_misfit(1 - parity, other_ref, targets_ref)
    across = rows_of(1 - parity, other_ref.shape[0])
    square_ref[...] = jnp.sum(mine * mine + theirs * theirs, axis=0, keepdims=True)
    cross_ref[...] = -jnp.sum(mine * wanted + theirs * needed, axis=0, keepdims=True)
    best = None
    for step in range(high_ref.shape[1] // chunk):
        part = slice(step * chunk, (step + 1) * chunk)
        turn = jnp.abs(turn_ref[:, part] + backward(high_ref[across, part], low_ref[across, part], turned))
        for k in range(chunk // LANE):
            piece = turn[:, k * LANE : (k + 1) * LANE]
            best = piece if best is None else jnp.maximum(best, piece)
    half = peak_ref.shape[0] // 2
    peak_ref[:half] = jnp.broadcast_to(jnp.max(best.T, axis=0, keepdims=True), (half, LANE))
    peak_ref[half:] = jnp.broadcast_to(mass_ref[...], (half, LANE))


def cols(ref, index):
    return ref.at[:, pl.ds(pl.multiple_of(index * LANE, LANE), LANE)]


def cut(ref, first, count, index):
    return ref.at[first : first + count, pl.ds(pl.multiple_of(index * LANE, LANE), LANE)]


def sides(source, edge, blocks, parity):
    left = (source >= 0) & (source < edge)
    right = source >= edge + blocks
    inner = jnp.where(left, source, source - edge - blocks)
    near_side = (left & (parity == 1)) | (right & (parity == 0))
    far_side = (left & (parity == 0)) | (right & (parity == 1))
    return inner, near_side, far_side


def tabulate(me_ref, drop_ref, dest_ref, near_ref, far_ref, table_ref):
    blocks = drop_ref.shape[0]
    slots = table_ref.shape[0]
    edge = (slots - blocks) // 2
    me = me_ref[0]
    near = jnp.max(near_ref[near_ref.shape[0] - 8 :, :LANE]).astype(jnp.int32)
    far = jnp.max(far_ref[far_ref.shape[0] - 8 :, :LANE]).astype(jnp.int32)
    before = jnp.where((me & 1) == 1, near, far)
    after = jnp.where((me & 1) == 1, far, near)
    for slot in range(slots):
        table_ref[slot] = jnp.int32(-1)
    count = jnp.int32(0)
    for cand in range(slots):
        if cand < edge:
            here = (before >> cand) & 1
        elif cand < edge + blocks:
            k = cand - edge
            here = jnp.where((drop_ref[k] == 0) & (dest_ref[k] == me), jnp.int32(1), jnp.int32(0))
        else:
            here = (after >> (cand - edge - blocks)) & 1

        @pl.when(here == 1)
        def _(cand=cand, count=count):
            table_ref[count] = jnp.int32(cand)

        count = count + here


def place_own(first, last, edge, blocks, parity, table_ref, near_ref, own_ref, out_ref, blank, sems):
    rows = out_ref.shape[0]
    blank[...] = jnp.zeros_like(blank)
    for slot in range(first, last):
        source = table_ref[slot]
        inner, near_side, _ = sides(source, edge, blocks, parity)

        @pl.when(source < 0)
        def _(slot=slot):
            pltpu.make_async_copy(blank, cols(out_ref, slot), sems.at[slot]).start()

        @pl.when((source >= edge) & (source < edge + blocks))
        def _(slot=slot, source=source):
            pltpu.make_async_copy(cols(own_ref, source - edge), cols(out_ref, slot), sems.at[slot]).start()

        @pl.when(near_side)
        def _(slot=slot, inner=inner):
            pltpu.make_async_copy(cut(near_ref, 0, rows, inner), cols(out_ref, slot), sems.at[slot]).start()

    for slot in range(first, last):
        far_side = sides(table_ref[slot], edge, blocks, parity)[2]

        @pl.when(jnp.logical_not(far_side))
        def _(slot=slot):
            pltpu.make_async_copy(blank, cols(out_ref, slot), sems.at[slot]).wait()


def place_a_kernel(me_ref, drop_ref, dest_ref, near_ref, far_ref, own_ref, out_ref, table_ref, blank, sems):
    slots = table_ref.shape[0]
    blocks = drop_ref.shape[0]
    tabulate(me_ref, drop_ref, dest_ref, near_ref, far_ref, table_ref)
    place_own(0, slots // 2, (slots - blocks) // 2, blocks, me_ref[0] & 1, table_ref, near_ref, own_ref, out_ref, blank, sems)


def place_b_kernel(edge, me_ref, table_ref, near_ref, own_ref, given_ref, out_ref, blank, sems):
    slots = table_ref.shape[0]
    place_own(slots // 2, slots, edge, slots - 2 * edge, me_ref[0] & 1, table_ref, near_ref, own_ref, out_ref, blank, sems)


def place_c_kernel(edge, me_ref, table_ref, far_a_ref, far_b_ref, given_ref, out_ref, sems):
    slots = table_ref.shape[0]
    half = out_ref.shape[0] // 2
    parity = me_ref[0] & 1

    def each(slot, inner):
        return [
            pltpu.make_async_copy(cut(ref, 0, half, inner), cut(out_ref, k * half, half, slot), sems.at[k, slot])
            for k, ref in enumerate((far_a_ref, far_b_ref))
        ]

    for slot in range(slots):
        inner, _, far_side = sides(table_ref[slot], edge, slots - 2 * edge, parity)

        @pl.when(far_side)
        def _(slot=slot, inner=inner):
            for copy in each(slot, inner):
                copy.start()

    for slot in range(slots):
        far_side = sides(table_ref[slot], edge, slots - 2 * edge, parity)[2]

        @pl.when(far_side)
        def _(slot=slot):
            for copy in each(slot, 0):
                copy.wait()


def place_coef_kernel(edge, me_ref, table_ref, near_ref, own_ref, far_ref, out_ref, blank, sems):
    slots = table_ref.shape[0]
    own = slots - 2 * edge
    parity = me_ref[0] & 1
    blank[...] = jnp.zeros_like(blank)

    def rows(ref, index):
        return ref.at[pl.ds(pl.multiple_of(index * LANE, LANE), LANE), :]

    def copy(slot, src):
        return pltpu.make_async_copy(src, rows(out_ref, slot), sems.at[slot])

    for slot in range(slots):
        source = table_ref[slot]
        left = (source >= 0) & (source < edge)
        right = source >= edge + own
        inner = jnp.where(left, source, source - edge - own)

        @pl.when(source < 0)
        def _(slot=slot):
            copy(slot, blank).start()

        @pl.when((source >= edge) & (source < edge + own))
        def _(slot=slot, source=source):
            copy(slot, rows(own_ref, source - edge)).start()

        @pl.when((left & (parity == 1)) | (right & (parity == 0)))
        def _(slot=slot, inner=inner):
            copy(slot, rows(near_ref, inner)).start()

        @pl.when((left & (parity == 0)) | (right & (parity == 1)))
        def _(slot=slot, inner=inner):
            copy(slot, rows(far_ref, inner)).start()

    for slot in range(slots):
        copy(slot, blank).wait()


VM = pltpu.MemorySpace.VMEM
SM = pltpu.MemorySpace.SMEM


def whole():
    return pl.BlockSpec(memory_space=VM)


def scalars():
    return pl.BlockSpec(memory_space=SM)


def f32(*shape):
    return jax.ShapeDtypeStruct(shape, jnp.float32)


def body(design, targets, coef_now, coef_prev, penalty, drop_mask, dest_shard):
    samples, feats = design.shape
    width = targets.shape[1]
    shards = lax.axis_size(AXIS)
    me = lax.axis_index(AXIS).astype(jnp.int32).reshape(1)
    lipschitz = (math.sqrt(samples) + math.sqrt(feats * shards)) ** 2
    first_push = (START - 1) / (START + 2)
    second_push = START / (START + 3)
    blocks = feats // LANE
    edge = blocks // 4
    slots = blocks + 2 * edge
    chunk = edge * LANE
    steps = feats // chunk
    half = samples // 2
    bits = stages(shards)

    params = pltpu.CompilerParams(vmem_limit_bytes=24 << 20)
    line = penalty.reshape(1, width)
    anywhere = pl.BlockSpec(memory_space=pl.ANY)

    def in_hbm(value):
        return pltpu.with_memory_space_constraint(value, pltpu.MemorySpace.HBM)

    def b16(*shape):
        return jax.ShapeDtypeStruct(shape, jnp.bfloat16)

    drop, dest = in_hbm(drop_mask), in_hbm(dest_shard)
    keep, send, near, far_a, far_b, held, high, low, base, point = pl.pallas_call(
        functools.partial(first_kernel, first_push, shards, chunk),
        in_specs=[scalars()] * 3 + [anywhere] * 3,
        out_specs=[whole()] * 10,
        out_shape=[
            f32(half, width), f32(half, width), f32(samples + 8, chunk), f32(half + 8, chunk), f32(half, chunk),
            f32(samples, feats), b16(samples, feats), b16(samples, feats), f32(feats, width), f32(feats, width),
        ],
        scratch_shapes=[
            pltpu.VMEM((feats, width), jnp.float32),
            pltpu.VMEM((samples, width), jnp.float32),
            pltpu.SemaphoreType.DMA((3, steps)),
        ],
        compiler_params=params,
        name="first",
    )(me, drop, dest, in_hbm(design), in_hbm(coef_now), in_hbm(coef_prev))

    def inward(value):
        return swap(value, 1)

    def outward(value):
        pairs = [(i, (i + 1) % shards if i % 2 else (i - 1) % shards) for i in range(shards)]
        return lax.ppermute(value, AXIS, pairs)

    even_bits = bits[-1:] + bits[1:-1]
    odd_bits = bits[2:] + bits[1:2]

    def combine(keep, send):
        total = keep + swap(send, 1)
        for even, odd in zip(even_bits, odd_bits):
            pairs = [(i, i ^ (odd if i % 2 else even)) for i in range(shards)]
            total = total + lax.ppermute(total, AXIS, pairs)
        other = swap(total, 1)
        turn = pl.pallas_call(
            functools.partial(half_kernel, chunk),
            in_specs=[scalars()] + [whole()] * 4,
            out_specs=whole(),
            out_shape=f32(width, feats),
            compiler_params=params,
            name="half",
        )(me, high, low, total, targets)
        return total, other, turn

    near_in = inward(near)
    far_a_in = outward(far_a)
    far_b_in = outward(far_b)

    sum_scratch = pltpu.VMEM((samples, width), jnp.float32)

    def descend(ahead, point, base, turn, other):
        out_shape = [f32(feats, width), f32(half, width), f32(half, width)]
        if ahead is None:
            out_shape += [f32(1, width), f32(chunk, width), f32(chunk, width)]
        else:
            out_shape += [f32(feats, width)]
        return pl.pallas_call(
            functools.partial(descend_kernel, ahead, chunk, lipschitz, samples / lipschitz),
            in_specs=[scalars()] + [whole()] * 8,
            out_specs=[whole()] * len(out_shape),
            out_shape=out_shape,
            scratch_shapes=[sum_scratch, pltpu.VMEM((feats, 2 * width), jnp.bfloat16)],
            compiler_params=params,
            name="descend",
        )(me, high, low, point, base, turn, other, targets, line)

    own, other, turn = combine(keep, send)
    coef_one, keep, send, point = descend(second_push, point, base, turn, other)
    own, other, turn = combine(keep, send)
    coef_two, keep, send, mass, near, far = descend(None, point, coef_one, turn, other)
    near_coef = inward(near)
    far_coef = outward(far)
    own, other, turn = combine(keep, send)

    blank = pltpu.VMEM((samples, LANE), jnp.float32)
    out_form = f32(samples, slots * LANE)
    design_out, table = pl.pallas_call(
        place_a_kernel,
        in_specs=[scalars()] * 3 + [whole()] * 3,
        out_specs=[anywhere, scalars()],
        out_shape=[out_form, jax.ShapeDtypeStruct((slots,), jnp.int32)],
        scratch_shapes=[blank, pltpu.SemaphoreType.DMA((slots,))],
        compiler_params=params,
        name="place_a",
    )(me, drop, dest, near_in, far_a_in, held)
    design_out = pl.pallas_call(
        functools.partial(place_b_kernel, edge),
        in_specs=[scalars()] * 2 + [whole()] * 2 + [anywhere],
        out_specs=anywhere,
        out_shape=out_form,
        scratch_shapes=[blank, pltpu.SemaphoreType.DMA((slots,))],
        input_output_aliases={4: 0},
        compiler_params=params,
        name="place_b",
    )(me, table, near_in, held, design_out)
    design_out = pl.pallas_call(
        functools.partial(place_c_kernel, edge),
        in_specs=[scalars()] * 2 + [whole()] * 2 + [anywhere],
        out_specs=anywhere,
        out_shape=out_form,
        scratch_shapes=[pltpu.SemaphoreType.DMA((2, slots))],
        input_output_aliases={4: 0},
        compiler_params=params,
        name="place_c",
    )(me, table, far_a_in, far_b_in, design_out)

    tail, square, cross = pl.pallas_call(
        functools.partial(peak_kernel, chunk),
        in_specs=[scalars()] + [whole()] * 7,
        out_specs=[whole()] * 3,
        out_shape=[f32(16, width), f32(1, width), f32(1, width)],
        compiler_params=params,
        name="peak",
    )(me, high, low, turn, own, other, targets, mass)
    is_peak = lax.broadcasted_iota(jnp.int32, (16, width), 0) < 8
    for bit in bits:
        got = swap(tail, bit)
        tail = jnp.where(is_peak, jnp.maximum(tail, got), tail + got)

    coef_out = pl.pallas_call(
        functools.partial(place_coef_kernel, edge),
        in_specs=[scalars(), scalars(), whole(), whole(), whole()],
        out_specs=anywhere,
        out_shape=f32(slots * LANE, width),
        scratch_shapes=[pltpu.VMEM((LANE, width), jnp.float32), pltpu.SemaphoreType.DMA((slots,))],
        compiler_params=params,
        name="place_coef",
    )(me, table, near_coef, coef_two, far_coef)

    peak, mass = tail[0], tail[8]
    dual_scale = jnp.maximum(penalty, peak / samples)
    ratio = penalty / dual_scale
    dual_value = (2.0 * ratio * cross[0] - ratio * ratio * square[0]) / (2.0 * samples)
    duality_gap = square[0] / (2.0 * samples) + penalty * mass - dual_value
    return (coef_out, design_out, duality_gap, dual_value, mass)


def solution(mesh):
    placed = (
        P("groups", "feat"),
        P("groups", None),
        P(("groups", "feat"), None),
        P(("groups", "feat"), None),
        P("groups"),
        P(("groups", "feat")),
        P(("groups", "feat")),
    )
    return jax.shard_map(
        body,
        mesh=mesh,
        in_specs=placed,
        out_specs=(
            P(("groups", "feat"), None),
            P("groups", "feat"),
            P("groups"),
            P("groups"),
            P("groups"),
        ),
        check_vma=False,
    )
```

```python
import functools
import math

import jax
import jax.numpy as jnp
from jax import lax
from jax.experimental import pallas as pl
from jax.experimental.pallas import tpu as pltpu
from jax.sharding import PartitionSpec as P


START = 40
LANE = 128
AXIS = "feat"


def swap(value, bit):
    count = lax.axis_size(AXIS)
    return lax.ppermute(value, AXIS, [(i, i ^ bit) for i in range(count)])


def stages(count):
    return [1 << s for s in range(count.bit_length() - 1)]


def halves(values):
    high = values.astype(jnp.bfloat16)
    low = (values - high.astype(jnp.float32)).astype(jnp.bfloat16)
    return high, low


def mul(left, right):
    return lax.dot_general(left, right, (((1,), (0,)), ((), ())), preferred_element_type=jnp.float32)


def shrink(values, level):
    return values - jnp.clip(values, -level, level)


def split_of(point):
    return jnp.concatenate(halves(point), axis=1)


def forward(high, low, split):
    width = split.shape[1] // 2
    both = mul(high, split)
    return both[:, :width] + both[:, width:] + mul(low, split[:, :width])


def backward(high, low, turned):
    width = turned.shape[0] // 2
    both = mul(turned, high)
    return both[:width] + both[width:] + mul(turned[:width], low)


def rows_of(side, half):
    return pl.ds(pl.multiple_of(side * half, half), half)


def turned_misfit(side, sum_ref, targets_ref):
    half = sum_ref.shape[0]
    wanted = targets_ref[rows_of(side, half), :]
    misfit = sum_ref[...] - wanted
    high, low = halves(misfit.T)
    return misfit, wanted, jnp.concatenate([high, low], axis=0)


def keep_kernel(me_ref, high_ref, low_ref, split_ref, keep_ref):
    rows = rows_of(me_ref[0] & 1, keep_ref.shape[0])
    keep_ref[...] = forward(high_ref[rows, :], low_ref[rows, :], split_ref[...])


def half_kernel(chunk, me_ref, high_ref, low_ref, own_ref, targets_ref, turn_ref):
    side = me_ref[0] & 1
    _, _, turned = turned_misfit(side, own_ref, targets_ref)
    rows = rows_of(side, own_ref.shape[0])
    for step in range(high_ref.shape[1] // chunk):
        part = slice(step * chunk, (step + 1) * chunk)
        turn_ref[:, part] = backward(high_ref[rows, part], low_ref[rows, part], turned)


def mask_of(drop_ref, dest_ref, start, count, shard):
    mask = jnp.int32(0)
    for k in range(count):
        moves = (drop_ref[start + k] == 0) & (dest_ref[start + k] == shard)
        mask = mask + jnp.where(moves, jnp.int32(1 << k), jnp.int32(0))
    return mask


def first_kernel(
    push, shards, chunk, me_ref, drop_ref, dest_ref, design_ref, now_ref, prev_ref,
    send_ref, split_ref, near_ref, far_a_ref, far_b_ref, held_ref, high_ref, low_ref, base_ref, point_ref,
    prev, sems,
):
    me = me_ref[0]
    parity = me & 1
    rows, feats = design_ref.shape
    blocks = drop_ref.shape[0]
    edge = chunk // LANE
    steps = feats // chunk
    across = rows_of(1 - parity, send_ref.shape[0])

    def copies(step):
        part = pl.ds(step * chunk, chunk)
        return [
            pltpu.make_async_copy(design_ref.at[:, part], held_ref.at[:, part], sems.at[0, step]),
            pltpu.make_async_copy(now_ref.at[part, :], base_ref.at[part, :], sems.at[1, step]),
            pltpu.make_async_copy(prev_ref.at[part, :], prev.at[part, :], sems.at[2, step]),
        ]

    for step in range(steps):
        for copy in copies(step):
            copy.start()
    for step in range(steps):
        for copy in copies(step):
            copy.wait()
        part = slice(step * chunk, (step + 1) * chunk)
        high, low = halves(held_ref[:, part])
        high_ref[:, part] = high
        low_ref[:, part] = low
        now = base_ref[part, :]
        point = now + push * (now - prev[part, :])
        point_ref[part, :] = point
        split_ref[part, :] = split_of(point)
        ahead = forward(high_ref[across, part], low_ref[across, part], split_ref[part, :])
        if step == 0:
            send_ref[...] = ahead
        else:
            send_ref[...] += ahead

    def put(right, near):
        block = held_ref[:, feats - chunk :] if right else held_ref[:, :chunk]
        if right:
            mask = mask_of(drop_ref, dest_ref, blocks - edge, edge, lax.rem(me + 1, shards))
        else:
            mask = mask_of(drop_ref, dest_ref, 0, edge, lax.rem(me + shards - 1, shards))
        ref = near_ref if near else far_a_ref
        if near:
            near_ref[:rows, :] = block
        else:
            far_a_ref[: rows // 2, :] = block[: rows // 2]
            far_b_ref[...] = block[rows // 2 :]
        ref[ref.shape[0] - 8 :, :] = jnp.full((8, chunk), mask.astype(jnp.float32), jnp.float32)

    @pl.when(parity == 1)
    def _():
        put(False, True)
        put(True, False)

    @pl.when(parity == 0)
    def _():
        put(True, True)
        put(False, False)


def descend_kernel(
    ahead, chunk, scale, level_scale, me_ref, high_ref, low_ref, point_ref, base_ref, turn_ref, other_ref, targets_ref,
    penalty_ref, coef_ref, send_ref, split_ref, *rest,
):
    parity = me_ref[0] & 1
    _, feats = high_ref.shape
    width = targets_ref.shape[1]
    _, _, turned = turned_misfit(1 - parity, other_ref, targets_ref)
    across = rows_of(1 - parity, other_ref.shape[0])
    level = penalty_ref[...] * level_scale
    mass = jnp.zeros((1, width), jnp.float32)
    for step in range(feats // chunk):
        part = slice(step * chunk, (step + 1) * chunk)
        turn = turn_ref[:, part] + backward(high_ref[across, part], low_ref[across, part], turned)
        coef = shrink(point_ref[part, :] - turn.T * (1.0 / scale), level)
        coef_ref[part, :] = coef
        if ahead is not None:
            coef = coef + ahead * (coef - base_ref[part, :])
            rest[0][part, :] = coef
        else:
            mass = mass + jnp.sum(jnp.abs(coef), axis=0, keepdims=True)
        split_ref[part, :] = split_of(coef)
    send_ref[...] = forward(high_ref[across, :], low_ref[across, :], split_ref[...])
    if ahead is None:
        mass_ref, near_ref, far_ref = rest[:3]
        mass_ref[...] = mass

        @pl.when(parity == 1)
        def _():
            near_ref[...] = coef_ref[: near_ref.shape[0], :]
            far_ref[...] = coef_ref[feats - far_ref.shape[0] :, :]

        @pl.when(parity == 0)
        def _():
            far_ref[...] = coef_ref[: far_ref.shape[0], :]
            near_ref[...] = coef_ref[feats - near_ref.shape[0] :, :]


def peak_kernel(
    chunk, me_ref, high_ref, low_ref, turn_ref, own_ref, other_ref, targets_ref, mass_ref, peak_ref, square_ref, cross_ref,
):
    parity = me_ref[0] & 1
    mine, wanted, _ = turned_misfit(parity, own_ref, targets_ref)
    theirs, needed, turned = turned_misfit(1 - parity, other_ref, targets_ref)
    across = rows_of(1 - parity, other_ref.shape[0])
    square_ref[...] = jnp.sum(mine * mine + theirs * theirs, axis=0, keepdims=True)
    cross_ref[...] = -jnp.sum(mine * wanted + theirs * needed, axis=0, keepdims=True)
    best = None
    for step in range(high_ref.shape[1] // chunk):
        part = slice(step * chunk, (step + 1) * chunk)
        turn = jnp.abs(turn_ref[:, part] + backward(high_ref[across, part], low_ref[across, part], turned))
        for k in range(chunk // LANE):
            piece = turn[:, k * LANE : (k + 1) * LANE]
            best = piece if best is None else jnp.maximum(best, piece)
    half = peak_ref.shape[0] // 2
    peak_ref[:half] = jnp.broadcast_to(jnp.max(best.T, axis=0, keepdims=True), (half, LANE))
    peak_ref[half:] = jnp.broadcast_to(mass_ref[...], (half, LANE))


def cols(ref, index):
    return ref.at[:, pl.ds(pl.multiple_of(index * LANE, LANE), LANE)]


def cut(ref, first, count, index):
    return ref.at[first : first + count, pl.ds(pl.multiple_of(index * LANE, LANE), LANE)]


def sides(source, edge, blocks, parity):
    left = (source >= 0) & (source < edge)
    right = source >= edge + blocks
    inner = jnp.where(left, source, source - edge - blocks)
    near_side = (left & (parity == 1)) | (right & (parity == 0))
    far_side = (left & (parity == 0)) | (right & (parity == 1))
    return inner, near_side, far_side


def tabulate(me_ref, drop_ref, dest_ref, near_ref, far_ref, table_ref):
    blocks = drop_ref.shape[0]
    slots = table_ref.shape[0]
    edge = (slots - blocks) // 2
    me = me_ref[0]
    near = jnp.max(near_ref[near_ref.shape[0] - 8 :, :LANE]).astype(jnp.int32)
    far = jnp.max(far_ref[far_ref.shape[0] - 8 :, :LANE]).astype(jnp.int32)
    before = jnp.where((me & 1) == 1, near, far)
    after = jnp.where((me & 1) == 1, far, near)
    for slot in range(slots):
        table_ref[slot] = jnp.int32(-1)
    count = jnp.int32(0)
    for cand in range(slots):
        if cand < edge:
            here = (before >> cand) & 1
        elif cand < edge + blocks:
            k = cand - edge
            here = jnp.where((drop_ref[k] == 0) & (dest_ref[k] == me), jnp.int32(1), jnp.int32(0))
        else:
            here = (after >> (cand - edge - blocks)) & 1

        @pl.when(here == 1)
        def _(cand=cand, count=count):
            table_ref[count] = jnp.int32(cand)

        count = count + here


def place_own(first, last, edge, blocks, parity, table_ref, near_ref, own_ref, out_ref, blank, sems):
    rows = out_ref.shape[0]
    blank[...] = jnp.zeros_like(blank)
    for slot in range(first, last):
        source = table_ref[slot]
        inner, near_side, _ = sides(source, edge, blocks, parity)

        @pl.when(source < 0)
        def _(slot=slot):
            pltpu.make_async_copy(blank, cols(out_ref, slot), sems.at[slot]).start()

        @pl.when((source >= edge) & (source < edge + blocks))
        def _(slot=slot, source=source):
            pltpu.make_async_copy(cols(own_ref, source - edge), cols(out_ref, slot), sems.at[slot]).start()

        @pl.when(near_side)
        def _(slot=slot, inner=inner):
            pltpu.make_async_copy(cut(near_ref, 0, rows, inner), cols(out_ref, slot), sems.at[slot]).start()

    for slot in range(first, last):
        far_side = sides(table_ref[slot], edge, blocks, parity)[2]

        @pl.when(jnp.logical_not(far_side))
        def _(slot=slot):
            pltpu.make_async_copy(blank, cols(out_ref, slot), sems.at[slot]).wait()


def place_a_kernel(me_ref, drop_ref, dest_ref, near_ref, far_ref, own_ref, out_ref, table_ref, blank, sems):
    slots = table_ref.shape[0]
    blocks = drop_ref.shape[0]
    tabulate(me_ref, drop_ref, dest_ref, near_ref, far_ref, table_ref)
    place_own(0, slots // 2, (slots - blocks) // 2, blocks, me_ref[0] & 1, table_ref, near_ref, own_ref, out_ref, blank, sems)


def place_b_kernel(edge, me_ref, table_ref, near_ref, own_ref, given_ref, out_ref, blank, sems):
    slots = table_ref.shape[0]
    place_own(slots // 2, slots, edge, slots - 2 * edge, me_ref[0] & 1, table_ref, near_ref, own_ref, out_ref, blank, sems)


def place_c_kernel(edge, me_ref, table_ref, far_a_ref, far_b_ref, given_ref, out_ref, sems):
    slots = table_ref.shape[0]
    half = out_ref.shape[0] // 2
    parity = me_ref[0] & 1

    def each(slot, inner):
        return [
            pltpu.make_async_copy(cut(ref, 0, half, inner), cut(out_ref, k * half, half, slot), sems.at[k, slot])
            for k, ref in enumerate((far_a_ref, far_b_ref))
        ]

    for slot in range(slots):
        inner, _, far_side = sides(table_ref[slot], edge, slots - 2 * edge, parity)

        @pl.when(far_side)
        def _(slot=slot, inner=inner):
            for copy in each(slot, inner):
                copy.start()

    for slot in range(slots):
        far_side = sides(table_ref[slot], edge, slots - 2 * edge, parity)[2]

        @pl.when(far_side)
        def _(slot=slot):
            for copy in each(slot, 0):
                copy.wait()


def place_coef_kernel(edge, me_ref, table_ref, near_ref, own_ref, far_ref, out_ref, blank, sems):
    slots = table_ref.shape[0]
    own = slots - 2 * edge
    parity = me_ref[0] & 1
    blank[...] = jnp.zeros_like(blank)

    def rows(ref, index):
        return ref.at[pl.ds(pl.multiple_of(index * LANE, LANE), LANE), :]

    def copy(slot, src):
        return pltpu.make_async_copy(src, rows(out_ref, slot), sems.at[slot])

    for slot in range(slots):
        source = table_ref[slot]
        left = (source >= 0) & (source < edge)
        right = source >= edge + own
        inner = jnp.where(left, source, source - edge - own)

        @pl.when(source < 0)
        def _(slot=slot):
            copy(slot, blank).start()

        @pl.when((source >= edge) & (source < edge + own))
        def _(slot=slot, source=source):
            copy(slot, rows(own_ref, source - edge)).start()

        @pl.when((left & (parity == 1)) | (right & (parity == 0)))
        def _(slot=slot, inner=inner):
            copy(slot, rows(near_ref, inner)).start()

        @pl.when((left & (parity == 0)) | (right & (parity == 1)))
        def _(slot=slot, inner=inner):
            copy(slot, rows(far_ref, inner)).start()

    for slot in range(slots):
        copy(slot, blank).wait()


VM = pltpu.MemorySpace.VMEM
SM = pltpu.MemorySpace.SMEM


def whole():
    return pl.BlockSpec(memory_space=VM)


def scalars():
    return pl.BlockSpec(memory_space=SM)


def f32(*shape):
    return jax.ShapeDtypeStruct(shape, jnp.float32)


def body(design, targets, coef_now, coef_prev, penalty, drop_mask, dest_shard):
    samples, feats = design.shape
    width = targets.shape[1]
    shards = lax.axis_size(AXIS)
    me = lax.axis_index(AXIS).astype(jnp.int32).reshape(1)
    lipschitz = (math.sqrt(samples) + math.sqrt(feats * shards)) ** 2
    first_push = (START - 1) / (START + 2)
    second_push = START / (START + 3)
    blocks = feats // LANE
    edge = blocks // 4
    slots = blocks + 2 * edge
    chunk = edge * LANE
    steps = feats // chunk
    half = samples // 2
    bits = stages(shards)

    params = pltpu.CompilerParams(vmem_limit_bytes=24 << 20)
    line = penalty.reshape(1, width)
    anywhere = pl.BlockSpec(memory_space=pl.ANY)

    def in_hbm(value):
        return pltpu.with_memory_space_constraint(value, pltpu.MemorySpace.HBM)

    def b16(*shape):
        return jax.ShapeDtypeStruct(shape, jnp.bfloat16)

    drop, dest = in_hbm(drop_mask), in_hbm(dest_shard)
    send, split, near, far_a, far_b, held, high, low, base, point = pl.pallas_call(
        functools.partial(first_kernel, first_push, shards, chunk),
        in_specs=[scalars()] * 3 + [anywhere] * 3,
        out_specs=[whole()] * 10,
        out_shape=[
            f32(half, width), b16(feats, 2 * width), f32(samples + 8, chunk), f32(half + 8, chunk), f32(half, chunk),
            f32(samples, feats), b16(samples, feats), b16(samples, feats), f32(feats, width), f32(feats, width),
        ],
        scratch_shapes=[
            pltpu.VMEM((feats, width), jnp.float32),
            pltpu.SemaphoreType.DMA((3, steps)),
        ],
        compiler_params=params,
        name="first",
    )(me, drop, dest, in_hbm(design), in_hbm(coef_now), in_hbm(coef_prev))

    def inward(value):
        return swap(value, 1)

    def outward(value):
        pairs = [(i, (i + 1) % shards if i % 2 else (i - 1) % shards) for i in range(shards)]
        return lax.ppermute(value, AXIS, pairs)

    even_bits = bits[-1:] + bits[1:-1]
    odd_bits = bits[2:] + bits[1:2]

    def combine(split, send):
        got = swap(send, 1)
        keep = pl.pallas_call(
            keep_kernel,
            in_specs=[scalars()] + [whole()] * 3,
            out_specs=whole(),
            out_shape=f32(half, width),
            compiler_params=params,
            name="keep",
        )(me, high, low, split)
        total = keep + got
        for even, odd in zip(even_bits, odd_bits):
            pairs = [(i, i ^ (odd if i % 2 else even)) for i in range(shards)]
            total = total + lax.ppermute(total, AXIS, pairs)
        other = swap(total, 1)
        turn = pl.pallas_call(
            functools.partial(half_kernel, chunk),
            in_specs=[scalars()] + [whole()] * 4,
            out_specs=whole(),
            out_shape=f32(width, feats),
            compiler_params=params,
            name="half",
        )(me, high, low, total, targets)
        return total, other, turn

    near_in = inward(near)
    far_a_in = outward(far_a)
    far_b_in = outward(far_b)


    def descend(ahead, point, base, turn, other):
        out_shape = [f32(feats, width), f32(half, width), b16(feats, 2 * width)]
        if ahead is None:
            out_shape += [f32(1, width), f32(chunk, width), f32(chunk, width)]
        else:
            out_shape += [f32(feats, width)]
        return pl.pallas_call(
            functools.partial(descend_kernel, ahead, chunk, lipschitz, samples / lipschitz),
            in_specs=[scalars()] + [whole()] * 8,
            out_specs=[whole()] * len(out_shape),
            out_shape=out_shape,
            compiler_params=params,
            name="descend",
        )(me, high, low, point, base, turn, other, targets, line)

    own, other, turn = combine(split, send)
    coef_one, send, split, point = descend(second_push, point, base, turn, other)
    own, other, turn = combine(split, send)
    coef_two, send, split, mass, near, far = descend(None, point, coef_one, turn, other)
    near_coef = inward(near)
    far_coef = outward(far)
    own, other, turn = combine(split, send)

    blank = pltpu.VMEM((samples, LANE), jnp.float32)
    out_form = f32(samples, slots * LANE)
    design_out, table = pl.pallas_call(
        place_a_kernel,
        in_specs=[scalars()] * 3 + [whole()] * 3,
        out_specs=[anywhere, scalars()],
        out_shape=[out_form, jax.ShapeDtypeStruct((slots,), jnp.int32)],
        scratch_shapes=[blank, pltpu.SemaphoreType.DMA((slots,))],
        compiler_params=params,
        name="place_a",
    )(me, drop, dest, near_in, far_a_in, held)
    design_out = pl.pallas_call(
        functools.partial(place_b_kernel, edge),
        in_specs=[scalars()] * 2 + [whole()] * 2 + [anywhere],
        out_specs=anywhere,
        out_shape=out_form,
        scratch_shapes=[blank, pltpu.SemaphoreType.DMA((slots,))],
        input_output_aliases={4: 0},
        compiler_params=params,
        name="place_b",
    )(me, table, near_in, held, design_out)
    design_out = pl.pallas_call(
        functools.partial(place_c_kernel, edge),
        in_specs=[scalars()] * 2 + [whole()] * 2 + [anywhere],
        out_specs=anywhere,
        out_shape=out_form,
        scratch_shapes=[pltpu.SemaphoreType.DMA((2, slots))],
        input_output_aliases={4: 0},
        compiler_params=params,
        name="place_c",
    )(me, table, far_a_in, far_b_in, design_out)

    tail, square, cross = pl.pallas_call(
        functools.partial(peak_kernel, chunk),
        in_specs=[scalars()] + [whole()] * 7,
        out_specs=[whole()] * 3,
        out_shape=[f32(16, width), f32(1, width), f32(1, width)],
        compiler_params=params,
        name="peak",
    )(me, high, low, turn, own, other, targets, mass)
    is_peak = lax.broadcasted_iota(jnp.int32, (16, width), 0) < 8
    for bit in bits:
        got = swap(tail, bit)
        tail = jnp.where(is_peak, jnp.maximum(tail, got), tail + got)

    coef_out = pl.pallas_call(
        functools.partial(place_coef_kernel, edge),
        in_specs=[scalars(), scalars(), whole(), whole(), whole()],
        out_specs=anywhere,
        out_shape=f32(slots * LANE, width),
        scratch_shapes=[pltpu.VMEM((LANE, width), jnp.float32), pltpu.SemaphoreType.DMA((slots,))],
        compiler_params=params,
        name="place_coef",
    )(me, table, near_coef, coef_two, far_coef)

    peak, mass = tail[0], tail[8]
    dual_scale = jnp.maximum(penalty, peak / samples)
    ratio = penalty / dual_scale
    dual_value = (2.0 * ratio * cross[0] - ratio * ratio * square[0]) / (2.0 * samples)
    duality_gap = square[0] / (2.0 * samples) + penalty * mass - dual_value
    return (coef_out, design_out, duality_gap, dual_value, mass)


def solution(mesh):
    placed = (
        P("groups", "feat"),
        P("groups", None),
        P(("groups", "feat"), None),
        P(("groups", "feat"), None),
        P("groups"),
        P(("groups", "feat")),
        P(("groups", "feat")),
    )
    return jax.shard_map(
        body,
        mesh=mesh,
        in_specs=placed,
        out_specs=(
            P(("groups", "feat"), None),
            P("groups", "feat"),
            P("groups"),
            P("groups"),
            P("groups"),
        ),
        check_vma=False,
    )
```

```python
import functools
import math

import jax
import jax.numpy as jnp
from jax import lax
from jax.experimental import pallas as pl
from jax.experimental.pallas import tpu as pltpu
from jax.sharding import PartitionSpec as P


START = 40
LANE = 128
AXIS = "feat"


def swap(value, bit):
    count = lax.axis_size(AXIS)
    return lax.ppermute(value, AXIS, [(i, i ^ bit) for i in range(count)])


def stages(count):
    return [1 << s for s in range(count.bit_length() - 1)]


def halves(values):
    high = values.astype(jnp.bfloat16)
    low = (values - high.astype(jnp.float32)).astype(jnp.bfloat16)
    return high, low


def mul(left, right):
    return lax.dot_general(left, right, (((1,), (0,)), ((), ())), preferred_element_type=jnp.float32)


def shrink(values, level):
    return values - jnp.clip(values, -level, level)


def split_of(point):
    return jnp.concatenate(halves(point), axis=1)


def forward(high, low, split):
    width = split.shape[1] // 2
    both = mul(high, split)
    return both[:, :width] + both[:, width:] + mul(low, split[:, :width])


def backward(high, low, turned):
    width = turned.shape[0] // 2
    both = mul(turned, high)
    return both[:width] + both[width:] + mul(turned[:width], low)


def rows_of(side, half):
    return pl.ds(pl.multiple_of(side * half, half), half)


def turned_misfit(side, sum_ref, targets_ref):
    half = sum_ref.shape[0]
    wanted = targets_ref[rows_of(side, half), :]
    misfit = sum_ref[...] - wanted
    high, low = halves(misfit.T)
    return misfit, wanted, jnp.concatenate([high, low], axis=0)


def keep_kernel(me_ref, high_ref, low_ref, split_ref, keep_ref):
    rows = rows_of(me_ref[0] & 1, keep_ref.shape[0])
    keep_ref[...] = forward(high_ref[rows, :], low_ref[rows, :], split_ref[...])


def half_kernel(chunk, me_ref, high_ref, low_ref, own_ref, targets_ref, turn_ref):
    side = me_ref[0] & 1
    _, _, turned = turned_misfit(side, own_ref, targets_ref)
    rows = rows_of(side, own_ref.shape[0])
    for step in range(high_ref.shape[1] // chunk):
        part = slice(step * chunk, (step + 1) * chunk)
        turn_ref[:, part] = backward(high_ref[rows, part], low_ref[rows, part], turned)


def mask_of(drop_ref, dest_ref, start, count, shard):
    mask = jnp.int32(0)
    for k in range(count):
        moves = (drop_ref[start + k] == 0) & (dest_ref[start + k] == shard)
        mask = mask + jnp.where(moves, jnp.int32(1 << k), jnp.int32(0))
    return mask


def first_kernel(
    push, chunk, me_ref, design_ref, now_ref, prev_ref,
    send_ref, split_ref, held_ref, high_ref, low_ref, base_ref, point_ref,
    prev, sems,
):
    me = me_ref[0]
    parity = me & 1
    _, feats = design_ref.shape
    steps = feats // chunk
    across = rows_of(1 - parity, send_ref.shape[0])

    def copies(step):
        part = pl.ds(step * chunk, chunk)
        return [
            pltpu.make_async_copy(design_ref.at[:, part], held_ref.at[:, part], sems.at[0, step]),
            pltpu.make_async_copy(now_ref.at[part, :], base_ref.at[part, :], sems.at[1, step]),
            pltpu.make_async_copy(prev_ref.at[part, :], prev.at[part, :], sems.at[2, step]),
        ]

    for step in range(steps):
        for copy in copies(step):
            copy.start()
    for step in range(steps):
        for copy in copies(step):
            copy.wait()
        part = slice(step * chunk, (step + 1) * chunk)
        high, low = halves(held_ref[:, part])
        high_ref[:, part] = high
        low_ref[:, part] = low
        now = base_ref[part, :]
        point = now + push * (now - prev[part, :])
        point_ref[part, :] = point
        split_ref[part, :] = split_of(point)
        ahead = forward(high_ref[across, part], low_ref[across, part], split_ref[part, :])
        if step == 0:
            send_ref[...] = ahead
        else:
            send_ref[...] += ahead


def edges_kernel(shards, me_ref, drop_ref, dest_ref, held_ref, near_ref, far_a_ref, far_b_ref):
    me = me_ref[0]
    parity = me & 1
    rows, feats = held_ref.shape
    chunk = near_ref.shape[1]
    edge = chunk // LANE
    blocks = drop_ref.shape[0]

    def put(right, near):
        block = held_ref[:, feats - chunk :] if right else held_ref[:, :chunk]
        if right:
            mask = mask_of(drop_ref, dest_ref, blocks - edge, edge, lax.rem(me + 1, shards))
        else:
            mask = mask_of(drop_ref, dest_ref, 0, edge, lax.rem(me + shards - 1, shards))
        ref = near_ref if near else far_a_ref
        if near:
            near_ref[:rows, :] = block
        else:
            far_a_ref[: rows // 2, :] = block[: rows // 2]
            far_b_ref[...] = block[rows // 2 :]
        ref[ref.shape[0] - 8 :, :] = jnp.full((8, chunk), mask.astype(jnp.float32), jnp.float32)

    @pl.when(parity == 1)
    def _():
        put(False, True)
        put(True, False)

    @pl.when(parity == 0)
    def _():
        put(True, True)
        put(False, False)


def descend_kernel(
    ahead, chunk, scale, level_scale, me_ref, high_ref, low_ref, point_ref, base_ref, turn_ref, other_ref, targets_ref,
    penalty_ref, coef_ref, send_ref, split_ref, *rest,
):
    parity = me_ref[0] & 1
    _, feats = high_ref.shape
    width = targets_ref.shape[1]
    _, _, turned = turned_misfit(1 - parity, other_ref, targets_ref)
    across = rows_of(1 - parity, other_ref.shape[0])
    level = penalty_ref[...] * level_scale
    mass = jnp.zeros((1, width), jnp.float32)
    for step in range(feats // chunk):
        part = slice(step * chunk, (step + 1) * chunk)
        turn = turn_ref[:, part] + backward(high_ref[across, part], low_ref[across, part], turned)
        coef = shrink(point_ref[part, :] - turn.T * (1.0 / scale), level)
        coef_ref[part, :] = coef
        if ahead is not None:
            coef = coef + ahead * (coef - base_ref[part, :])
            rest[0][part, :] = coef
        else:
            mass = mass + jnp.sum(jnp.abs(coef), axis=0, keepdims=True)
        split_ref[part, :] = split_of(coef)
    send_ref[...] = forward(high_ref[across, :], low_ref[across, :], split_ref[...])
    if ahead is None:
        mass_ref, near_ref, far_ref = rest[:3]
        mass_ref[...] = mass

        @pl.when(parity == 1)
        def _():
            near_ref[...] = coef_ref[: near_ref.shape[0], :]
            far_ref[...] = coef_ref[feats - far_ref.shape[0] :, :]

        @pl.when(parity == 0)
        def _():
            far_ref[...] = coef_ref[: far_ref.shape[0], :]
            near_ref[...] = coef_ref[feats - near_ref.shape[0] :, :]


def peak_kernel(
    chunk, me_ref, high_ref, low_ref, turn_ref, own_ref, other_ref, targets_ref, mass_ref, peak_ref, square_ref, cross_ref,
):
    parity = me_ref[0] & 1
    mine, wanted, _ = turned_misfit(parity, own_ref, targets_ref)
    theirs, needed, turned = turned_misfit(1 - parity, other_ref, targets_ref)
    across = rows_of(1 - parity, other_ref.shape[0])
    square_ref[...] = jnp.sum(mine * mine + theirs * theirs, axis=0, keepdims=True)
    cross_ref[...] = -jnp.sum(mine * wanted + theirs * needed, axis=0, keepdims=True)
    best = None
    for step in range(high_ref.shape[1] // chunk):
        part = slice(step * chunk, (step + 1) * chunk)
        turn = jnp.abs(turn_ref[:, part] + backward(high_ref[across, part], low_ref[across, part], turned))
        for k in range(chunk // LANE):
            piece = turn[:, k * LANE : (k + 1) * LANE]
            best = piece if best is None else jnp.maximum(best, piece)
    half = peak_ref.shape[0] // 2
    peak_ref[:half] = jnp.broadcast_to(jnp.max(best.T, axis=0, keepdims=True), (half, LANE))
    peak_ref[half:] = jnp.broadcast_to(mass_ref[...], (half, LANE))


def cols(ref, index):
    return ref.at[:, pl.ds(pl.multiple_of(index * LANE, LANE), LANE)]


def cut(ref, first, count, index):
    return ref.at[first : first + count, pl.ds(pl.multiple_of(index * LANE, LANE), LANE)]


def sides(source, edge, blocks, parity):
    left = (source >= 0) & (source < edge)
    right = source >= edge + blocks
    inner = jnp.where(left, source, source - edge - blocks)
    near_side = (left & (parity == 1)) | (right & (parity == 0))
    far_side = (left & (parity == 0)) | (right & (parity == 1))
    return inner, near_side, far_side


def tabulate(me_ref, drop_ref, dest_ref, near_ref, far_ref, table_ref):
    blocks = drop_ref.shape[0]
    slots = table_ref.shape[0]
    edge = (slots - blocks) // 2
    me = me_ref[0]
    near = jnp.max(near_ref[near_ref.shape[0] - 8 :, :LANE]).astype(jnp.int32)
    far = jnp.max(far_ref[far_ref.shape[0] - 8 :, :LANE]).astype(jnp.int32)
    before = jnp.where((me & 1) == 1, near, far)
    after = jnp.where((me & 1) == 1, far, near)
    for slot in range(slots):
        table_ref[slot] = jnp.int32(-1)
    count = jnp.int32(0)
    for cand in range(slots):
        if cand < edge:
            here = (before >> cand) & 1
        elif cand < edge + blocks:
            k = cand - edge
            here = jnp.where((drop_ref[k] == 0) & (dest_ref[k] == me), jnp.int32(1), jnp.int32(0))
        else:
            here = (after >> (cand - edge - blocks)) & 1

        @pl.when(here == 1)
        def _(cand=cand, count=count):
            table_ref[count] = jnp.int32(cand)

        count = count + here


def place_own(first, last, edge, blocks, parity, table_ref, near_ref, own_ref, out_ref, blank, sems):
    rows = out_ref.shape[0]
    blank[...] = jnp.zeros_like(blank)
    for slot in range(first, last):
        source = table_ref[slot]
        inner, near_side, _ = sides(source, edge, blocks, parity)

        @pl.when(source < 0)
        def _(slot=slot):
            pltpu.make_async_copy(blank, cols(out_ref, slot), sems.at[slot]).start()

        @pl.when((source >= edge) & (source < edge + blocks))
        def _(slot=slot, source=source):
            pltpu.make_async_copy(cols(own_ref, source - edge), cols(out_ref, slot), sems.at[slot]).start()

        @pl.when(near_side)
        def _(slot=slot, inner=inner):
            pltpu.make_async_copy(cut(near_ref, 0, rows, inner), cols(out_ref, slot), sems.at[slot]).start()

    for slot in range(first, last):
        far_side = sides(table_ref[slot], edge, blocks, parity)[2]

        @pl.when(jnp.logical_not(far_side))
        def _(slot=slot):
            pltpu.make_async_copy(blank, cols(out_ref, slot), sems.at[slot]).wait()


def place_a_kernel(me_ref, drop_ref, dest_ref, near_ref, far_ref, own_ref, out_ref, table_ref, blank, sems):
    slots = table_ref.shape[0]
    blocks = drop_ref.shape[0]
    tabulate(me_ref, drop_ref, dest_ref, near_ref, far_ref, table_ref)
    place_own(0, slots // 2, (slots - blocks) // 2, blocks, me_ref[0] & 1, table_ref, near_ref, own_ref, out_ref, blank, sems)


def place_b_kernel(edge, me_ref, table_ref, near_ref, own_ref, given_ref, out_ref, blank, sems):
    slots = table_ref.shape[0]
    place_own(slots // 2, slots, edge, slots - 2 * edge, me_ref[0] & 1, table_ref, near_ref, own_ref, out_ref, blank, sems)


def place_c_kernel(edge, me_ref, table_ref, far_a_ref, far_b_ref, given_ref, out_ref, sems):
    slots = table_ref.shape[0]
    half = out_ref.shape[0] // 2
    parity = me_ref[0] & 1

    def each(slot, inner):
        return [
            pltpu.make_async_copy(cut(ref, 0, half, inner), cut(out_ref, k * half, half, slot), sems.at[k, slot])
            for k, ref in enumerate((far_a_ref, far_b_ref))
        ]

    for slot in range(slots):
        inner, _, far_side = sides(table_ref[slot], edge, slots - 2 * edge, parity)

        @pl.when(far_side)
        def _(slot=slot, inner=inner):
            for copy in each(slot, inner):
                copy.start()

    for slot in range(slots):
        far_side = sides(table_ref[slot], edge, slots - 2 * edge, parity)[2]

        @pl.when(far_side)
        def _(slot=slot):
            for copy in each(slot, 0):
                copy.wait()


def place_coef_kernel(edge, me_ref, table_ref, near_ref, own_ref, far_ref, out_ref, blank, sems):
    slots = table_ref.shape[0]
    own = slots - 2 * edge
    parity = me_ref[0] & 1
    blank[...] = jnp.zeros_like(blank)

    def rows(ref, index):
        return ref.at[pl.ds(pl.multiple_of(index * LANE, LANE), LANE), :]

    def copy(slot, src):
        return pltpu.make_async_copy(src, rows(out_ref, slot), sems.at[slot])

    for slot in range(slots):
        source = table_ref[slot]
        left = (source >= 0) & (source < edge)
        right = source >= edge + own
        inner = jnp.where(left, source, source - edge - own)

        @pl.when(source < 0)
        def _(slot=slot):
            copy(slot, blank).start()

        @pl.when((source >= edge) & (source < edge + own))
        def _(slot=slot, source=source):
            copy(slot, rows(own_ref, source - edge)).start()

        @pl.when((left & (parity == 1)) | (right & (parity == 0)))
        def _(slot=slot, inner=inner):
            copy(slot, rows(near_ref, inner)).start()

        @pl.when((left & (parity == 0)) | (right & (parity == 1)))
        def _(slot=slot, inner=inner):
            copy(slot, rows(far_ref, inner)).start()

    for slot in range(slots):
        copy(slot, blank).wait()


VM = pltpu.MemorySpace.VMEM
SM = pltpu.MemorySpace.SMEM


def whole():
    return pl.BlockSpec(memory_space=VM)


def scalars():
    return pl.BlockSpec(memory_space=SM)


def f32(*shape):
    return jax.ShapeDtypeStruct(shape, jnp.float32)


def body(design, targets, coef_now, coef_prev, penalty, drop_mask, dest_shard):
    samples, feats = design.shape
    width = targets.shape[1]
    shards = lax.axis_size(AXIS)
    me = lax.axis_index(AXIS).astype(jnp.int32).reshape(1)
    lipschitz = (math.sqrt(samples) + math.sqrt(feats * shards)) ** 2
    first_push = (START - 1) / (START + 2)
    second_push = START / (START + 3)
    blocks = feats // LANE
    edge = blocks // 4
    slots = blocks + 2 * edge
    chunk = edge * LANE
    steps = feats // chunk
    half = samples // 2
    bits = stages(shards)

    params = pltpu.CompilerParams(vmem_limit_bytes=24 << 20)
    line = penalty.reshape(1, width)
    anywhere = pl.BlockSpec(memory_space=pl.ANY)

    def in_hbm(value):
        return pltpu.with_memory_space_constraint(value, pltpu.MemorySpace.HBM)

    def b16(*shape):
        return jax.ShapeDtypeStruct(shape, jnp.bfloat16)

    drop, dest = in_hbm(drop_mask), in_hbm(dest_shard)
    send, split, held, high, low, base, point = pl.pallas_call(
        functools.partial(first_kernel, first_push, chunk),
        in_specs=[scalars()] + [anywhere] * 3,
        out_specs=[whole()] * 7,
        out_shape=[
            f32(half, width), b16(feats, 2 * width),
            f32(samples, feats), b16(samples, feats), b16(samples, feats), f32(feats, width), f32(feats, width),
        ],
        scratch_shapes=[
            pltpu.VMEM((feats, width), jnp.float32),
            pltpu.SemaphoreType.DMA((3, steps)),
        ],
        compiler_params=params,
        name="first",
    )(me, in_hbm(design), in_hbm(coef_now), in_hbm(coef_prev))
    near, far_a, far_b = pl.pallas_call(
        functools.partial(edges_kernel, shards),
        in_specs=[scalars()] * 3 + [whole()],
        out_specs=[whole()] * 3,
        out_shape=[f32(samples + 8, chunk), f32(half + 8, chunk), f32(half, chunk)],
        compiler_params=params,
        name="edges",
    )(me, drop, dest, held)

    def inward(value):
        return swap(value, 1)

    def outward(value):
        pairs = [(i, (i + 1) % shards if i % 2 else (i - 1) % shards) for i in range(shards)]
        return lax.ppermute(value, AXIS, pairs)

    even_bits = bits[-1:] + bits[1:-1]
    odd_bits = bits[2:] + bits[1:2]

    def combine(split, send):
        got = swap(send, 1)
        keep = pl.pallas_call(
            keep_kernel,
            in_specs=[scalars()] + [whole()] * 3,
            out_specs=whole(),
            out_shape=f32(half, width),
            compiler_params=params,
            name="keep",
        )(me, high, low, split)
        total = keep + got
        for even, odd in zip(even_bits, odd_bits):
            pairs = [(i, i ^ (odd if i % 2 else even)) for i in range(shards)]
            total = total + lax.ppermute(total, AXIS, pairs)
        other = swap(total, 1)
        turn = pl.pallas_call(
            functools.partial(half_kernel, chunk),
            in_specs=[scalars()] + [whole()] * 4,
            out_specs=whole(),
            out_shape=f32(width, feats),
            compiler_params=params,
            name="half",
        )(me, high, low, total, targets)
        return total, other, turn

    near_in = inward(near)
    far_a_in = outward(far_a)
    far_b_in = outward(far_b)


    def descend(ahead, point, base, turn, other):
        out_shape = [f32(feats, width), f32(half, width), b16(feats, 2 * width)]
        if ahead is None:
            out_shape += [f32(1, width), f32(chunk, width), f32(chunk, width)]
        else:
            out_shape += [f32(feats, width)]
        return pl.pallas_call(
            functools.partial(descend_kernel, ahead, chunk, lipschitz, samples / lipschitz),
            in_specs=[scalars()] + [whole()] * 8,
            out_specs=[whole()] * len(out_shape),
            out_shape=out_shape,
            compiler_params=params,
            name="descend",
        )(me, high, low, point, base, turn, other, targets, line)

    own, other, turn = combine(split, send)
    coef_one, send, split, point = descend(second_push, point, base, turn, other)
    own, other, turn = combine(split, send)
    coef_two, send, split, mass, near, far = descend(None, point, coef_one, turn, other)
    near_coef = inward(near)
    far_coef = outward(far)
    own, other, turn = combine(split, send)

    blank = pltpu.VMEM((samples, LANE), jnp.float32)
    out_form = f32(samples, slots * LANE)
    design_out, table = pl.pallas_call(
        place_a_kernel,
        in_specs=[scalars()] * 3 + [whole()] * 3,
        out_specs=[anywhere, scalars()],
        out_shape=[out_form, jax.ShapeDtypeStruct((slots,), jnp.int32)],
        scratch_shapes=[blank, pltpu.SemaphoreType.DMA((slots,))],
        compiler_params=params,
        name="place_a",
    )(me, drop, dest, near_in, far_a_in, held)
    design_out = pl.pallas_call(
        functools.partial(place_b_kernel, edge),
        in_specs=[scalars()] * 2 + [whole()] * 2 + [anywhere],
        out_specs=anywhere,
        out_shape=out_form,
        scratch_shapes=[blank, pltpu.SemaphoreType.DMA((slots,))],
        input_output_aliases={4: 0},
        compiler_params=params,
        name="place_b",
    )(me, table, near_in, held, design_out)
    design_out = pl.pallas_call(
        functools.partial(place_c_kernel, edge),
        in_specs=[scalars()] * 2 + [whole()] * 2 + [anywhere],
        out_specs=anywhere,
        out_shape=out_form,
        scratch_shapes=[pltpu.SemaphoreType.DMA((2, slots))],
        input_output_aliases={4: 0},
        compiler_params=params,
        name="place_c",
    )(me, table, far_a_in, far_b_in, design_out)

    tail, square, cross = pl.pallas_call(
        functools.partial(peak_kernel, chunk),
        in_specs=[scalars()] + [whole()] * 7,
        out_specs=[whole()] * 3,
        out_shape=[f32(16, width), f32(1, width), f32(1, width)],
        compiler_params=params,
        name="peak",
    )(me, high, low, turn, own, other, targets, mass)
    is_peak = lax.broadcasted_iota(jnp.int32, (16, width), 0) < 8
    for bit in bits:
        got = swap(tail, bit)
        tail = jnp.where(is_peak, jnp.maximum(tail, got), tail + got)

    coef_out = pl.pallas_call(
        functools.partial(place_coef_kernel, edge),
        in_specs=[scalars(), scalars(), whole(), whole(), whole()],
        out_specs=anywhere,
        out_shape=f32(slots * LANE, width),
        scratch_shapes=[pltpu.VMEM((LANE, width), jnp.float32), pltpu.SemaphoreType.DMA((slots,))],
        compiler_params=params,
        name="place_coef",
    )(me, table, near_coef, coef_two, far_coef)

    peak, mass = tail[0], tail[8]
    dual_scale = jnp.maximum(penalty, peak / samples)
    ratio = penalty / dual_scale
    dual_value = (2.0 * ratio * cross[0] - ratio * ratio * square[0]) / (2.0 * samples)
    duality_gap = square[0] / (2.0 * samples) + penalty * mass - dual_value
    return (coef_out, design_out, duality_gap, dual_value, mass)


def solution(mesh):
    placed = (
        P("groups", "feat"),
        P("groups", None),
        P(("groups", "feat"), None),
        P(("groups", "feat"), None),
        P("groups"),
        P(("groups", "feat")),
        P(("groups", "feat")),
    )
    return jax.shard_map(
        body,
        mesh=mesh,
        in_specs=placed,
        out_specs=(
            P(("groups", "feat"), None),
            P("groups", "feat"),
            P("groups"),
            P("groups"),
            P("groups"),
        ),
        check_vma=False,
    )
```
